128 devices in a mesh: seq: 16 (over x, y), head: 8 (over z, core).
Axes of the slice: x: 4, y: 4, z: 4, core: 2. Of those that a mesh axis runs over, the one named last changes fastest.
Arguments:
- tokens: bfloat16 [8192, 1024], P('seq'), may hold values from -6 to 6
- attn_gain: float32 [1024], replicated, may hold values from 0.5 to 1.5
- w_query: bfloat16 [1024, 1024], P(None, 'head'), may hold values from -0.25 to 0.25
- key_weight: bfloat16 [1024, 512], P(None, 'head'), may hold values from -0.25 to 0.25
- value_weight: bfloat16 [1024, 512], P(None, 'head'), may hold values from -0.1875 to 0.1875
- w_out: bfloat16 [1024, 1024], P('head'), may hold values from -0.75 to 0.75
- moe_gain: float32 [1024], replicated, may hold values from 0.5 to 1.5
- w_router: bfloat16 [1024, 32], replicated, may hold values from -0.046875 to 0.046875
- w_gate_up: bfloat16 [32, 1024, 1024], P('head'), may hold values from -0.1875 to 0.1875
- w_down: bfloat16 [32, 512, 1024], P('head'), may hold values from -0.25 to 0.25
- expert_ids: int32 [8192, 8], P('seq'), may hold values from 0 to 31, all different within a row; in each aligned block of 512 rows (0 to 511, 512 to 1023, ...) at most 256 rows name the same one
- source_cache_pages: bfloat16 [1024, 8, 8192], P('seq', 'head'), may hold values from -6 to 6
- req_pages: int32 [16, 16], replicated, may hold values from 1 to 8, as said below
- req_dest: int32 [16, 16], replicated, may hold values from 0 to 15, as said below
Outputs:
- layer_out: bfloat16 [8192, 1024], P('seq')
- relaid_pages: bfloat16 [2048, 8, 8192], P('seq', 'head')
The draws below stay inside these ranges and needn't reach their ends.
Inputs may be any that keep to these rules, and one draw needn't show every extreme that they name: `req_pages`: each source's requests hold in all at most 64 pages; exactly one request of each source holds 8 pages, the others fewer. `req_dest`: each row names every destination once; every source's request of 8 pages goes to one common destination. `expert_ids`: each row names 8 different experts; among the rows of one index of seq no expert is named more than 256 times.
All inputs are finite; a program needn't handle non-finite values.
Results may differ from the reference program's by a relative error of at most 0.024.
Values may be sent and summed in bfloat16 or wider, within the bound.
A program may use at most 128 MiB of HBM per device.

```python
import math
import jax
import jax.numpy as jnp
import numpy as np
from jax import lax

MODEL_DIM = 1024
QUERY_HEADS = 16
KEY_VALUE_HEADS = 8
HEAD_DIM = 64
EXPERTS = 32
EFF = 512
TOPK = 8
TOK_DEV = 512
CACHE_PER_SEQ = 64
GROUPS = 8
HQ_DEV = 2
KVH_DEV = 1
EXP_DEV = 4
TOKENS = 8192
CAP = 256
REQ_DEV = 16
MAXP = 8
DEST_CAP = 128
PAGE_ENTRIES = 8192
N_SEQ = 16


def request_plan(key):
    base_key = jax.random.fold_in(key, 11)
    big_key, weight_key, hot_key, order_key = jax.random.split(base_key, 4)
    longest = jax.random.randint(big_key, (N_SEQ,), 0, REQ_DEV)
    request_ids = jnp.arange(REQ_DEV, dtype=jnp.int32)
    is_other = request_ids[None, :] != longest[:, None]
    weights = jax.random.randint(weight_key, (N_SEQ, REQ_DEV), 0, 4)
    weights = jnp.where(is_other, weights * weights * weights + 1, 0)
    spare_pages = CACHE_PER_SEQ - MAXP - (REQ_DEV - 1)
    shares = spare_pages * weights // jnp.sum(weights, axis=1, keepdims=True)
    page_counts = jnp.where(is_other, jnp.minimum(1 + shares, MAXP - 1), MAXP)
    hot_dest = jax.random.randint(hot_key, (), 0, N_SEQ)
    orders = jax.vmap(lambda row_key: jax.random.permutation(row_key, N_SEQ))(jax.random.split(order_key, N_SEQ))
    at_longest = jnp.sum(jnp.where(is_other, 0, orders), axis=1, keepdims=True)
    destinations = jnp.where(is_other, jnp.where(orders == hot_dest, at_longest, orders), hot_dest)
    return (page_counts.astype(jnp.int32), destinations.astype(jnp.int32))


def draw_req_pages(key, part):
    return request_plan(key)[0]


def draw_req_dest(key, part):
    return request_plan(key)[1]


def steps_of(stream_key, shape, cuts, smallest, top_value):
    def one(dim, blocks):
        heights = jax.random.uniform(jax.random.fold_in(jax.random.fold_in(stream_key, 6), dim), (blocks,), jnp.float32, smallest / len(cuts), top_value / len(cuts))
        return jnp.repeat(jnp.exp(heights), shape[dim] // blocks).reshape((-1,) + (1,) * (len(shape) - dim - 1))

    loudness = one(*cuts[0])
    for cut in cuts[1:]:
        loudness = loudness * one(*cut)
    return loudness


def deal_out(key, own, number, rows, number_of, top, limit, lean):
    order = jax.random.permutation(key, number_of)
    crowded, ordinary = portions_of(number_of, rows * top, limit, lean, True), portions_of(number_of, rows * top, limit, lean, False)
    places = jnp.arange(number_of)

    def named(lengths, rotation):
        used = int((lengths > 0).sum())
        fixed = max(1, used // 4)
        passed = fixed + (places - fixed + rotation * (used - fixed)) % max(1, number_of - fixed)
        return jnp.zeros((number_of,), jnp.int32).at[order[jnp.where(places < fixed, places, passed)]].set(jnp.asarray(lengths, jnp.int32))

    lengths = jnp.where(number % 4 == 0, named(crowded, number // 4), named(ordinary, number - number // 4 - 1))
    mixed = jax.random.permutation(jax.random.fold_in(own, 3), number_of)
    donor, sink = mixed[0:number_of // 2 * 2:2], mixed[1:number_of // 2 * 2:2]
    slack = jnp.minimum(lengths[donor] - 1, limit - lengths[sink]) // 2
    slack = jnp.where((donor == order[0]) | (sink == order[0]) | (lengths[sink] == 0), 0, jnp.maximum(slack, 0))
    passed = jax.random.randint(jax.random.fold_in(own, 4), (number_of // 2,), 0, 1 << 20) % (slack + 1)
    lengths = lengths.at[donor].add(-passed).at[sink].add(passed)
    items = jnp.searchsorted(jnp.cumsum(lengths), jnp.arange(rows * top), side="right").astype(jnp.int32)
    table = items.reshape(top, rows).T
    table = table[jax.random.permutation(jax.random.fold_in(own, 1), rows)]
    rotation = jax.random.randint(jax.random.fold_in(own, 2), (rows, 1), 0, top)
    return jnp.take_along_axis(table, (jnp.arange(top)[None, :] + rotation) % top, axis=1)


def portions_of(count, total, reach, lean, full):
    loads = [(1 << 20) // math.isqrt(grade ** lean) + 1 for grade in range(1, count + 1)]
    largest = reach if full else min(reach, max(-(-total // count), total * loads[0] // sum(loads)))
    least = 1 if total - largest >= count - 1 else 0
    holding, spare = [largest] + [least] * (count - 1), total - largest - least * (count - 1)
    while spare > 0:
        candidates = [i for i in range(1, count) if holding[i] < largest] or [i for i in range(1, count) if holding[i] < reach]
        whole, left = sum([loads[i] for i in candidates]), spare
        for i in candidates:
            extra = min(reach - holding[i], max(1, left * loads[i] // whole), spare)
            holding[i] = holding[i] + extra
            spare = spare - extra
    return np.array(holding)


def noise(own_key, shape, scale, bound, pieces=(), kind=jnp.bfloat16):
    factor_of = steps_of(own_key, shape, pieces, -0.22, 0.18) if pieces else 1.0
    result = jax.random.normal(own_key, shape, jnp.float32) * scale * factor_of
    return jnp.minimum(jnp.maximum(result, -bound), bound).astype(kind)


def setup_inputs(seed: int = 0) -> dict:
    key_list = jax.random.split(jax.random.key(seed), 15)
    tokens = noise(key_list[0], (TOKENS, MODEL_DIM), 1.0, 6.0, ((0, 16),))
    attn_gain = jnp.clip(1.0 + 0.1 * jax.random.normal(key_list[1], (MODEL_DIM,), jnp.float32), 0.5, 1.5)
    w_query = noise(key_list[2], (MODEL_DIM, QUERY_HEADS * HEAD_DIM), (MODEL_DIM // 2) ** -0.5, 0.25, ((1, 8),))
    key_weight = noise(key_list[3], (MODEL_DIM, KEY_VALUE_HEADS * HEAD_DIM), (MODEL_DIM // 2) ** -0.5, 0.25, ((1, 8),))
    value_weight = noise(key_list[4], (MODEL_DIM, KEY_VALUE_HEADS * HEAD_DIM), MODEL_DIM ** -0.5, 0.1875, ((1, 8),))
    w_out = noise(key_list[5], (QUERY_HEADS * HEAD_DIM, MODEL_DIM), HEAD_DIM ** -0.5, 0.75, ((0, 8),))
    moe_gain = jnp.clip(1.0 + 0.1 * jax.random.normal(key_list[6], (MODEL_DIM,), jnp.float32), 0.5, 1.5)
    w_router = jnp.clip(jax.random.uniform(key_list[7], (MODEL_DIM, EXPERTS), jnp.float32, -0.046875, 0.046875), -0.046875, 0.046875).astype(jnp.bfloat16)
    w_gate_up = noise(key_list[8], (EXPERTS, MODEL_DIM, 2 * EFF), MODEL_DIM ** -0.5, 0.1875, ((0, 8),))
    w_down = noise(key_list[9], (EXPERTS, EFF, MODEL_DIM), EFF ** -0.5, 0.25, ((0, 8),))
    expert_ids_keys = jax.random.split(jax.random.fold_in(key_list[10], 1), TOKENS // TOK_DEV)
    expert_ids_turns = jax.random.permutation(jax.random.fold_in(key_list[10], 3), TOKENS // TOK_DEV)
    expert_ids = jax.vmap(lambda own, number: deal_out(jax.random.fold_in(key_list[10], 2), own, number, TOK_DEV, EXPERTS, TOPK, CAP, 1))(expert_ids_keys, expert_ids_turns).reshape((TOKENS, TOPK))
    source_cache_pages = noise(key_list[11], (N_SEQ * CACHE_PER_SEQ, KEY_VALUE_HEADS, PAGE_ENTRIES), 1.0, 6.0, ((0, 16), (1, 8)))
    req_pages = draw_req_pages(jax.random.fold_in(key_list[14], 71), 0)
    req_dest = draw_req_dest(jax.random.fold_in(key_list[14], 71), 0)
    return dict(tokens=tokens, attn_gain=attn_gain, w_query=w_query, key_weight=key_weight, value_weight=value_weight, w_out=w_out, moe_gain=moe_gain, w_router=w_router, w_gate_up=w_gate_up, w_down=w_down, expert_ids=expert_ids, source_cache_pages=source_cache_pages, req_pages=req_pages, req_dest=req_dest)


def rms_scale(row_data, gain_vec):
    values = row_data.astype(jnp.float32)
    return values * lax.rsqrt(lax.optimization_barrier(jnp.mean(values * values, axis=-1, keepdims=True)) + 1e-05) * gain_vec

def rotary(values, positions):
    half_dim = values.shape[-1] // 2
    frequency = 10000.0 ** (jnp.arange(half_dim, dtype=jnp.float32) * (-2.0 / values.shape[-1]))
    angles = positions.astype(jnp.float32)[:, None] * frequency[None, :]
    cosine = jnp.cos(angles)[:, None, :]
    sine_vals = jnp.sin(angles)[:, None, :]
    first_half = values[..., :half_dim]
    second_half = values[..., half_dim:]
    return jnp.concatenate([first_half * cosine - second_half * sine_vals, second_half * cosine + first_half * sine_vals], axis=-1)

def rounded(values):
    return lax.optimization_barrier(values.astype(jnp.bfloat16)).astype(jnp.float32)

def reference(tokens, attn_gain, w_query, key_weight, value_weight, w_out, moe_gain, w_router, w_gate_up, w_down, expert_ids, source_cache_pages, req_pages, req_dest):
    normed = rms_scale(tokens, attn_gain).astype(jnp.bfloat16)
    positions = jnp.arange(TOKENS, dtype=jnp.int32)
    block_len = math.gcd(TOKENS, 1024)
    block_count = TOKENS // block_len
    q_cols = HQ_DEV * HEAD_DIM
    kv_cols = KVH_DEV * HEAD_DIM
    query_group_size = QUERY_HEADS // KEY_VALUE_HEADS

    def group_term(total, group_index):
        w_q = lax.dynamic_slice_in_dim(w_query, group_index * q_cols, q_cols, 1)
        w_k = lax.dynamic_slice_in_dim(key_weight, group_index * kv_cols, kv_cols, 1)
        w_v = lax.dynamic_slice_in_dim(value_weight, group_index * kv_cols, kv_cols, 1)
        w_o = lax.dynamic_slice_in_dim(w_out, group_index * q_cols, q_cols, 0)
        queries = rotary(jnp.dot(normed, w_q, preferred_element_type=jnp.float32).reshape(TOKENS, HQ_DEV, HEAD_DIM), positions)
        queries = rounded(queries).reshape(TOKENS, KVH_DEV, query_group_size, HEAD_DIM)
        key_rows = rounded(rotary(jnp.dot(normed, w_k, preferred_element_type=jnp.float32).reshape(TOKENS, KVH_DEV, HEAD_DIM), positions))
        value_rows = rounded(jnp.dot(normed, w_v, preferred_element_type=jnp.float32)).reshape(TOKENS, KVH_DEV, HEAD_DIM)

        def one_block(block_index):
            q_start = (block_index * block_len).astype(jnp.int32)
            q_block = lax.dynamic_slice_in_dim(queries, q_start, block_len, 0)
            q_pos = q_start + jnp.arange(block_len, dtype=jnp.int32)

            def add_keys(key_index, carried):
                numerator, denominator = carried
                k_start = (key_index * block_len).astype(jnp.int32)
                key_block = lax.dynamic_slice_in_dim(key_rows, k_start, block_len, 0)
                value_block = lax.dynamic_slice_in_dim(value_rows, k_start, block_len, 0)
                k_pos = k_start + jnp.arange(block_len, dtype=jnp.int32)
                raw_scores = jnp.einsum('tkgd,skd->kgts', q_block, key_block) * 0.125
                capped = 30.0 * jnp.tanh(raw_scores / 30.0)
                allowed = k_pos[None, None, None, :] <= q_pos[None, None, :, None]
                weights = jnp.where(allowed, jnp.exp(capped), 0.0)
                denominator = denominator + lax.optimization_barrier(jnp.sum(weights, axis=-1))
                numerator = numerator + jnp.einsum('kgts,skd->kgtd', rounded(weights), value_block)
                return (numerator, denominator)
            start_state = (jnp.zeros((KVH_DEV, query_group_size, block_len, HEAD_DIM), jnp.float32), jnp.zeros((KVH_DEV, query_group_size, block_len), jnp.float32))
            numerator, denominator = lax.fori_loop(0, block_index + 1, add_keys, start_state)
            context = numerator / denominator[..., None]
            return jnp.transpose(context, (2, 0, 1, 3)).reshape(block_len, q_cols)
        context = lax.map(one_block, jnp.arange(block_count, dtype=jnp.int32)).reshape(TOKENS, q_cols).astype(jnp.bfloat16)
        partial_term = jnp.dot(context, w_o, preferred_element_type=jnp.float32)
        return (total + rounded(partial_term), None)
    attn_total, _ = lax.scan(group_term, jnp.zeros((TOKENS, MODEL_DIM), jnp.float32), jnp.arange(GROUPS, dtype=jnp.int32))
    hidden = (tokens.astype(jnp.float32) + attn_total).astype(jnp.bfloat16)
    moe_in = rms_scale(hidden, moe_gain).astype(jnp.bfloat16)
    logits = jnp.dot(moe_in, w_router, preferred_element_type=jnp.float32)
    chosen = jnp.take_along_axis(logits, expert_ids, axis=1)
    raised = jnp.exp(chosen)
    gate_weights = (raised / lax.optimization_barrier(jnp.sum(raised, axis=1, keepdims=True))).reshape(-1)
    flat_ids = expert_ids.reshape(-1)
    hit_room = N_SEQ * CAP

    def expert_term(moe_term, expert):
        hit_list = jnp.nonzero(flat_ids == expert, size=hit_room, fill_value=TOKENS * TOPK)[0].astype(jnp.int32)
        valid = hit_list < TOKENS * TOPK
        token_ids = jnp.minimum(hit_list // TOPK, TOKENS - 1)
        selected = jnp.take(moe_in, token_ids, axis=0)
        gate_up = jnp.dot(selected, w_gate_up[expert], preferred_element_type=jnp.float32)
        activated = (jax.nn.silu(gate_up[:, :EFF]) * gate_up[:, EFF:]).astype(jnp.bfloat16)
        expert_out = jnp.dot(activated, w_down[expert], preferred_element_type=jnp.float32).astype(jnp.bfloat16)
        scaling = jnp.where(valid, gate_weights[jnp.minimum(hit_list, TOKENS * TOPK - 1)], 0.0)
        return (moe_term.at[token_ids].add(scaling[:, None] * expert_out.astype(jnp.float32)), None)

    def group_moe(total, group_index):
        experts_here = group_index * EXP_DEV + jnp.arange(EXP_DEV, dtype=jnp.int32)
        group_sum, _ = lax.scan(expert_term, jnp.zeros((TOKENS, MODEL_DIM), jnp.float32), experts_here)
        return (total + rounded(group_sum), None)
    moe_total, _ = lax.scan(group_moe, jnp.zeros((TOKENS, MODEL_DIM), jnp.float32), jnp.arange(GROUPS, dtype=jnp.int32))
    layer_out = (hidden.astype(jnp.float32) + moe_total).astype(jnp.bfloat16)
    page_starts = (jnp.cumsum(req_pages, axis=1) - req_pages).astype(jnp.int32)
    sources = jnp.arange(N_SEQ, dtype=jnp.int32)

    def one_dest(dest_index):
        matched = req_dest == dest_index
        arrive_len = lax.optimization_barrier(jnp.sum(jnp.where(matched, req_pages, 0), axis=1)).astype(jnp.int32)
        arrive_begin = lax.optimization_barrier(jnp.sum(jnp.where(matched, page_starts, 0), axis=1)).astype(jnp.int32)
        arrive_off = (jnp.cumsum(arrive_len) - arrive_len).astype(jnp.int32)
        slot_ids = jnp.arange(DEST_CAP, dtype=jnp.int32)
        owner_ids = (lax.optimization_barrier(jnp.sum((arrive_off[None, :] <= slot_ids[:, None]).astype(jnp.int32), axis=1)) - 1).astype(jnp.int32)
        owner_hot = owner_ids[:, None] == sources[None, :]
        owner_off = lax.optimization_barrier(jnp.sum(jnp.where(owner_hot, arrive_off[None, :], 0), axis=1)).astype(jnp.int32)
        owner_begin = lax.optimization_barrier(jnp.sum(jnp.where(owner_hot, arrive_begin[None, :], 0), axis=1)).astype(jnp.int32)
        row_ids = owner_ids * CACHE_PER_SEQ + owner_begin + slot_ids - owner_off
        filled = slot_ids < jnp.sum(arrive_len)
        return jnp.where(filled, row_ids, N_SEQ * CACHE_PER_SEQ).astype(jnp.int32)
    row_list = lax.map(one_dest, sources).reshape(-1)
    padded_rows = jnp.concatenate([source_cache_pages, jnp.zeros((1, KEY_VALUE_HEADS, PAGE_ENTRIES), jnp.bfloat16)], axis=0)
    relaid_pages = jnp.take(padded_rows, row_list, axis=0)
    return (layer_out, relaid_pages)
```

```python
import functools

import jax
import jax.numpy as jnp
import numpy as np
from jax import lax
from jax.experimental import pallas as pl
from jax.experimental.pallas import tpu as pltpu
from jax.sharding import PartitionSpec as P

HD = 64
LANES = 128
COLS = 256
F32 = jnp.float32
BF16 = jnp.bfloat16
NT = (((1,), (1,)), ((), ()))


def rotary_tables(tokens, rows):
    lane_freq = np.arange(LANES) % (HD // 2)
    freq = 10000.0 ** (lane_freq * (-2.0 / HD))
    coarse = np.arange(tokens // rows)[:, None] * float(rows) * freq[None, :]
    fine = np.arange(rows)[:, None] * freq[None, :]
    table = [np.cos(coarse), np.sin(coarse), np.cos(fine), np.sin(fine)]
    return [part.astype(np.float32) for part in table]


def dot(a, b, dims=None):
    if dims is None:
        return jnp.dot(a, b, preferred_element_type=F32)
    return lax.dot_general(a, b, dims, preferred_element_type=F32)


def kernel(
    n_seq,
    tok_h, again_h, wq_h, wkt_h, wvt_h, wo_h, mgain_h, wrt_h, wgu_h, wd_h, ids_h, pages_h, rp_h, rd_h,
    cc_h, cs_h, fc_h, fs_h,
    out_h, relaid_h,
    tok, again, wq, wkvt, mgain, wrt, wgu, wd, ids, pages, rp, rd, cc, cs, fc, fs,
    woutg, normed, kvbuf, qbuf, qpack, qrecv, acc, part, prt, ctxg, hidden, moe, gcol, gb, act,
    p1s, keep, p1r, p2s, town, p2r, outb, psend, precv,
    sem_in, kv_s, kv_r, q_s, q_r, pt_s, pt_r, pg_s, pg_r, wo_s, wo_r, wo_f, cx_s, cx_r, cx_f,
    l1_s, l1_r, l2_s, l2_r, ag_s, ag_r, ag_f, out_sem,
):
    me = lax.axis_index("seq")
    hh = lax.axis_index("head")
    zz = hh // 2
    core = hh % 2
    mate = hh + 1 - 2 * core
    rows = tok.shape[0]
    half = rows // 2
    light = me < n_seq // 2
    last = n_seq - 1
    partner = last - me

    barrier = pltpu.get_barrier_semaphore()
    for k in range(1, n_seq):
        pl.semaphore_signal(barrier, inc=1, device_id={"seq": (me + k) % n_seq})
    for k in range(1, 8):
        pl.semaphore_signal(barrier, inc=1, device_id={"head": (hh + k) % 8})

    loads = [
        (tok_h, tok), (again_h, again), (wq_h, wq), (wkt_h, wkvt.at[pl.ds(0, HD)]),
        (wvt_h, wkvt.at[pl.ds(HD, HD)]), (cc_h, cc), (cs_h, cs), (fc_h, fc), (fs_h, fs),
        (pages_h, pages), (rp_h, rp), (rd_h, rd),
        (mgain_h, mgain), (wrt_h, wrt), (ids_h, ids),
    ]
    copies = [pltpu.make_async_copy(src, dst, sem_in.at[i]) for i, (src, dst) in enumerate(loads)]
    n0 = len(copies)
    big = [pltpu.make_async_copy(wo_h, woutg.at[pl.ds(hh * 128, 128)], sem_in.at[n0])]
    for e in range(4):
        big.append(pltpu.make_async_copy(wgu_h.at[e], wgu.at[e], sem_in.at[n0 + 1 + e]))
    big.append(pltpu.make_async_copy(wd_h, wd, sem_in.at[n0 + 5]))
    for c in copies:
        c.start()
    for c in big:
        c.start()

    for i in (0, 1):
        copies[i].wait()
    for r in range(0, rows, 128):
        x = tok[r : r + 128, :].astype(F32)
        scale = lax.rsqrt(jnp.mean(x * x, axis=1, keepdims=True) + 1e-05)
        normed[r : r + 128, :] = (x * scale * again[...]).astype(BF16)
    for i in range(2, 9):
        copies[i].wait()

    q = dot(normed[...], wq[...])
    kv = dot(normed[...], wkvt[...], NT)
    lane = lax.broadcasted_iota(jnp.int32, (64, LANES), 1)
    first = (lane % HD) < HD // 2
    low = lane < HD
    own_kv = kvbuf.at[me]
    ccb = cc[pl.ds(pl.multiple_of(me * 8, 8), 8), :]
    csb = cs[pl.ds(pl.multiple_of(me * 8, 8), 8), :]
    for g in range(rows // 64):
        ca = ccb[g : g + 1, :]
        sa = csb[g : g + 1, :]
        cosv = ca * fc[...] - sa * fs[...]
        sinv = sa * fc[...] + ca * fs[...]
        sinv = jnp.where(first, -sinv, sinv)
        sl = slice(g * 64, g * 64 + 64)
        qg = q[sl]
        kg = kv[sl]
        qsw = jnp.where(first, pltpu.roll(qg, 96, 1), pltpu.roll(qg, 32, 1))
        ksw = jnp.where(first, pltpu.roll(kg, 96, 1), pltpu.roll(kg, 32, 1))
        qr = qg * cosv + qsw * sinv
        kr = jnp.where(low, kg * cosv + ksw * sinv, kg)
        kvbuf[me, sl, :] = kr.astype(BF16)
        qpack[sl, :] = qr.astype(BF16)
        qbuf[0, 0, sl, :] = jnp.where(low, qr, 0.0).astype(BF16)
        qbuf[0, 1, sl, :] = jnp.where(low, pltpu.roll(qr, HD, 1), 0.0).astype(BF16)

    pl.semaphore_wait(barrier, n_seq - 1 + 7)

    def kv_copy(k):
        peer = (me + k) % n_seq
        needed = jnp.where(
            peer >= n_seq // 2,
            (peer - 8 <= me) & (me < peer),
            (me < peer) | (me <= 6 - peer),
        )
        return needed, pltpu.make_async_remote_copy(
            own_kv, kvbuf.at[me], kv_s.at[k], kv_r.at[me], device_id={"seq": peer}
        )

    for k in range(1, n_seq):
        needed, c = kv_copy(k)

        @pl.when(needed)
        def _(c=c):
            c.start()

    q_copy = pltpu.make_async_remote_copy(qpack, qrecv, q_s, q_r, device_id={"seq": partner})
    ships = me >= n_seq // 2 + 1
    helps = me <= n_seq // 2 - 2

    @pl.when(ships)
    def _():
        q_copy.start()

    peers = [((zz + d) % 4) * 2 + core for d in (1, 3, 2)]
    others = [((zz + d) % 4) * 2 + 1 - core for d in (0, 1, 3, 2)]

    def wo_copy(slot, src, dev, ss):
        return pltpu.make_async_remote_copy(
            src, woutg.at[pl.ds(slot * 128, 128)], ss, wo_r.at[slot], device_id={"head": dev}
        )

    wo_copies = [wo_copy(hh, wo_h, dev, wo_s.at[i]) for i, dev in enumerate(peers + [mate])]
    for c in wo_copies:
        c.start()

    for i in range(9, 12):
        copies[i].wait()
    srow = lax.broadcasted_iota(jnp.int32, (16, 16), 0)
    mine = srow == me
    own_pages = jnp.sum(jnp.where(mine, rp[...].astype(F32), 0.0), axis=0, keepdims=True)
    own_dest = jnp.sum(jnp.where(mine, rd[...].astype(F32), 0.0), axis=0, keepdims=True)
    slot = lax.broadcasted_iota(jnp.int32, (128, 16), 0)
    req = lax.broadcasted_iota(jnp.int32, (128, 16), 1).astype(F32)
    match = own_dest == (slot // 8).astype(F32)
    send_len = jnp.sum(jnp.where(match, own_pages, 0.0), axis=1, keepdims=True)
    send_req = jnp.sum(jnp.where(match, req, 0.0), axis=1, keepdims=True)
    send_start = jnp.sum(jnp.where(req < send_req, own_pages, 0.0), axis=1, keepdims=True)
    sub = (lax.broadcasted_iota(jnp.int32, (128, 64), 0) % 8).astype(F32)
    src_row = lax.broadcasted_iota(jnp.int32, (128, 64), 1).astype(F32)
    pack = jnp.where((src_row == send_start + sub) & (sub < send_len), 1.0, 0.0).astype(BF16)

    def pack_step(i, carry):
        cols = pl.ds(pl.multiple_of(i * 1024, 1024), 1024)
        psend[:, cols] = dot(pack, pages[:, cols]).astype(BF16)
        return carry

    lax.fori_loop(0, 8, pack_step, 0)
    pg_own = pltpu.make_async_copy(psend.at[pl.ds(me * 8, 8)], precv.at[pl.ds(me * 8, 8)], pg_s.at[0])
    pg_own.start()

    def pg_copy(k):
        peer = (me + k) % n_seq
        return pltpu.make_async_remote_copy(
            psend.at[pl.ds(peer * 8, 8)], precv.at[pl.ds(me * 8, 8)], pg_s.at[k], pg_r.at[me],
            device_id={"seq": peer},
        )

    for k in range(1, n_seq):
        pg_copy(k).start()

    def attend(w, h, r0, nr, kblk, v1, diag):
        qt = qbuf[w, h, r0 : r0 + nr, :]
        s = dot(qt, kblk, NT)
        wts = jnp.exp(30.0 * jnp.tanh(s * (1.0 / 240.0)))
        if diag:
            tri = lax.broadcasted_iota(jnp.int32, s.shape, 1) <= lax.broadcasted_iota(jnp.int32, s.shape, 0)
            wts = jnp.where(tri, wts, 0.0)
        return dot(wts.astype(BF16), v1)

    def ones_in(kv_part):
        keep_low = lax.broadcasted_iota(jnp.int32, kv_part.shape, 1) < HD
        return jnp.where(keep_low, jnp.ones_like(kv_part), kv_part)

    ka, kb = kvbuf[me, :half, :], kvbuf[me, half:, :]
    va, vb = ones_in(ka), ones_in(kb)
    for h in range(2):
        acc[0, h, :half, :] = attend(0, h, 0, half, ka, va, True)
        acc[0, h, half:, :] = attend(0, h, half, half, ka, va, False) + attend(0, h, half, half, kb, vb, True)
    acc[1] = jnp.zeros_like(acc[1])

    def block(w, b):
        kblk = kvbuf[b]
        v1 = ones_in(kblk)
        for h in range(2):
            for r0 in (0, half):
                acc[w, h, r0 : r0 + half, :] += attend(w, h, r0, half, kblk, v1, False)

    def kv_wait(b):
        pltpu.make_async_remote_copy(
            own_kv, kvbuf.at[b], kv_s.at[0], kv_r.at[b], device_id={"seq": partner}
        ).wait_recv()

    p_copy = pltpu.make_async_remote_copy(part, prt, pt_s, pt_r, device_id={"seq": partner})

    @pl.when(helps)
    def _():
        q_copy.wait_recv()
        qr = qrecv[...]
        low_q = lax.broadcasted_iota(jnp.int32, qr.shape, 1) < HD
        zero = jnp.zeros_like(qr)
        qbuf[1, 0] = jnp.where(low_q, qr, zero)
        qbuf[1, 1] = jnp.where(low_q, pltpu.roll(qr.astype(F32), HD, 1).astype(BF16), zero)

        def help_step(b, carry):
            @pl.when(b != me)
            def _():
                kv_wait(b)

            block(1, b)
            return carry

        lax.fori_loop(0, 7 - me, help_step, 0)
        part[...] = acc[1].astype(BF16)
        p_copy.start()

    first_own = jnp.where(light, 0, me - 8)

    def own_step(i, carry):
        b = first_own + i

        @pl.when(jnp.logical_not(light) | (b > 6 - me))
        def _():
            kv_wait(b)

        block(0, b)
        return carry

    lax.fori_loop(0, jnp.where(light, me, 8), own_step, 0)

    wo_fwd = []
    for i, p in enumerate(peers):
        wo_copy(p, wo_h, mate, wo_s.at[0]).wait_recv()
        c = wo_copy(p, woutg.at[pl.ds(p * 128, 128)], mate, wo_f.at[i])
        c.start()
        wo_fwd.append(c)

    @pl.when(ships)
    def _():
        p_copy.wait_recv()
        acc[0] = acc[0] + prt[...].astype(F32)

    low_c = lax.broadcasted_iota(jnp.int32, (rows, LANES), 1) < HD
    c0 = acc[0, 0] / pltpu.roll(acc[0, 0], HD, 1)
    c1 = acc[0, 1] / pltpu.roll(acc[0, 1], HD, 1)
    ctxg[hh] = jnp.where(low_c, pltpu.roll(c0, HD, 1), c1).astype(BF16)

    def cx_copy(slot, dev, ss):
        return pltpu.make_async_remote_copy(
            ctxg.at[slot], ctxg.at[slot], ss, cx_r.at[slot], device_id={"head": dev}
        )

    cx_copies = [cx_copy(hh, dev, cx_s.at[i]) for i, dev in enumerate(peers + [mate])]
    for c in cx_copies:
        c.start()
    big[0].wait()
    for i in range(12, 15):
        copies[i].wait()
    cx_fwd = []
    for i, p in enumerate(peers):
        cx_copy(p, mate, cx_s.at[0]).wait_recv()
        c = cx_copy(p, mate, cx_f.at[i])
        c.start()
        cx_fwd.append(c)
    for p in others:
        wo_copy(p, wo_h, mate, wo_s.at[0]).wait_recv()
    for p in others:
        cx_copy(p, mate, cx_s.at[0]).wait_recv()

    for r in (0, half):
        x = jnp.concatenate([ctxg[i, r : r + half, :] for i in range(8)], axis=1)
        hid = (tok[r : r + half, :].astype(F32) + dot(x, woutg[...])).astype(BF16)
        hidden[r : r + half, :] = hid
        hf = hid.astype(F32)
        scale = lax.rsqrt(jnp.mean(hf * hf, axis=1, keepdims=True) + 1e-05)
        moe[r : r + half, :] = (hf * scale * mgain[...]).astype(BF16)

    logits = dot(wrt[...], moe[...], NT)
    expert = lax.broadcasted_iota(jnp.int32, logits.shape, 0)
    chosen = expert == ids[0:1, :]
    for k in range(1, 8):
        chosen = chosen | (expert == ids[k : k + 1, :])
    raised = jnp.where(chosen, jnp.exp(logits), 0.0)
    gates = raised / jnp.sum(raised, axis=0, keepdims=True)
    gcol[...] = jnp.transpose(jnp.concatenate([gates, jnp.zeros((96, rows), F32)], axis=0))
    lane_r = lax.broadcasted_iota(jnp.int32, (rows, LANES), 1)
    for e in range(4):
        picked = jnp.sum(jnp.where(lane_r == hh * 4 + e, gcol[...], 0.0), axis=1, keepdims=True)
        gb[e] = jnp.broadcast_to(picked, (rows, LANES))

    for e in range(1, 6):
        big[e].wait()

    def expert_step(e, carry):
        gate2 = jnp.concatenate([gb[e], gb[e]], axis=1)
        for c in range(2):
            g = dot(moe[...], wgu[e, :, c * COLS : c * COLS + COLS])
            u = dot(moe[...], wgu[e, :, 512 + c * COLS : 512 + c * COLS + COLS])
            a = g / (1.0 + jnp.exp(-g)) * u * gate2
            act[:, pl.ds(pl.multiple_of(e * 512 + c * COLS, COLS), COLS)] = a.astype(BF16)
        return carry

    lax.fori_loop(0, 4, expert_step, 0)

    own_half = pl.ds(pl.multiple_of(core * half, half), half)
    mate_half = pl.ds(pl.multiple_of((1 - core) * half, half), half)
    quarter = half // 4
    own_rows = pl.ds(pl.multiple_of(core * half + zz * quarter, quarter), quarter)
    zpeers = [(zz + d) % 4 for d in (1, 3, 2)]

    def l1_copy(n):
        return pltpu.make_async_remote_copy(p1s.at[n], p1r.at[n], l1_s.at[n], l1_r.at[n], device_id={"head": mate})

    def l2_copy(n, i, src_z):
        return pltpu.make_async_remote_copy(
            p2s.at[n, pl.ds(zpeers[i] * quarter, quarter)], p2r.at[n, src_z], l2_s.at[n, i], l2_r.at[n, src_z],
            device_id={"head": peers[i]},
        )

    def ag_copy(n, h_src, dev, ss):
        at = pl.ds((h_src % 2) * half + (h_src // 2) * quarter, quarter)
        return pltpu.make_async_remote_copy(
            outb.at[n, at], outb.at[n, at], ss, ag_r.at[n, h_src], device_id={"head": dev}
        )

    def stage_down(n):
        wcol = wd[:, n * COLS : n * COLS + COLS]
        p1s[n] = dot(act[mate_half, :], wcol).astype(BF16)
        l1_copy(n).start()
        keep[n] = dot(act[own_half, :], wcol)

    def stage_sum(n):
        l1_copy(n).wait_recv()
        t = keep[n] + p1r[n].astype(F32)
        p2s[n] = t.astype(BF16)
        for i in range(3):
            l2_copy(n, i, zz).start()
        keep[n] = t

    def stage_final(n):
        t = keep[n, pl.ds(pl.multiple_of(zz * quarter, quarter), quarter), :]
        for i in range(3):
            l2_copy(n, i, zpeers[i]).wait_recv()
            t = t + p2r[n, zpeers[i]].astype(F32)
        t = t + hidden[own_rows, n * COLS : n * COLS + COLS].astype(F32)
        outb[n, own_rows, :] = t.astype(BF16)
        for i, dev in enumerate(peers + [mate]):
            ag_copy(n, hh, dev, ag_s.at[n, i]).start()

    def stage_forward(n):
        for i, p in enumerate(peers):
            ag_copy(n, p, mate, ag_s.at[n, 0]).wait_recv()
            ag_copy(n, p, mate, ag_f.at[n, i]).start()

    def stage_out(n):
        for p in others:
            ag_copy(n, p, mate, ag_s.at[n, 0]).wait_recv()
        pltpu.make_async_copy(outb.at[n], out_h.at[:, pl.ds(n * COLS, COLS)], out_sem.at[n]).start()

    stages = [stage_down, stage_sum, stage_final, stage_forward, stage_out]
    for t in range(4 + len(stages) - 1):
        for j, stage in enumerate(stages):
            if 0 <= t - j < 4:
                stage(t - j)

    len_m = jnp.sum(jnp.where(rd[...] == me, rp[...].astype(F32), 0.0), axis=1, keepdims=True)
    s_of = lax.broadcasted_iota(jnp.int32, (16, 128), 1) // 8
    s_row = lax.broadcasted_iota(jnp.int32, (16, 128), 0)
    len_c = jnp.sum(jnp.where(s_row == s_of, len_m, 0.0), axis=0, keepdims=True)
    off_c = jnp.sum(jnp.where(s_row < s_of, len_m, 0.0), axis=0, keepdims=True)
    to_row = lax.broadcasted_iota(jnp.int32, (128, 128), 0).astype(F32)
    sub_c = (lax.broadcasted_iota(jnp.int32, (128, 128), 1) % 8).astype(F32)
    place = jnp.where((to_row == off_c + sub_c) & (sub_c < len_c), 1.0, 0.0).astype(BF16)
    pg_own.wait()
    for k in range(1, n_seq):
        src = (me + k) % n_seq
        pltpu.make_async_remote_copy(
            psend.at[pl.ds(0, 8)], precv.at[pl.ds(src * 8, 8)], pg_s.at[k], pg_r.at[src], device_id={"seq": src}
        ).wait_recv()
    for k in range(1, n_seq):
        pg_copy(k).wait_send()

    def place_step(i, carry):
        cols = pl.ds(pl.multiple_of(i * 1024, 1024), 1024)
        psend[:, cols] = dot(place, precv[:, cols]).astype(BF16)
        return carry

    lax.fori_loop(0, 8, place_step, 0)
    relaid = pltpu.make_async_copy(psend, relaid_h, out_sem.at[4])
    relaid.start()

    for k in range(1, n_seq):
        needed, c = kv_copy(k)

        @pl.when(needed)
        def _(c=c):
            c.wait_send()

    @pl.when(ships)
    def _():
        q_copy.wait_send()

    @pl.when(helps)
    def _():
        p_copy.wait_send()

    for c in wo_copies + wo_fwd + cx_copies + cx_fwd:
        c.wait_send()
    for n in range(4):
        l1_copy(n).wait_send()
        for i in range(3):
            l2_copy(n, i, zz).wait_send()
            ag_copy(n, peers[i], mate, ag_f.at[n, i]).wait_send()
        for i, dev in enumerate(peers + [mate]):
            ag_copy(n, hh, dev, ag_s.at[n, i]).wait_send()
        pltpu.make_async_copy(outb.at[n], out_h.at[:, pl.ds(n * COLS, COLS)], out_sem.at[n]).wait()
    relaid.wait()


def per_device(
    n_seq, tokens, attn_gain, w_query, key_weight, value_weight, w_out, moe_gain, w_router, w_gate_up, w_down,
    expert_ids, source_cache_pages, req_pages, req_dest,
):
    rows, width = tokens.shape
    n_pages, _, entries = source_cache_pages.shape
    tables = rotary_tables(rows * n_seq, 64)
    half = rows // 2
    v = pltpu.VMEM
    scratch = [
        v((rows, width), BF16), v((1, width), F32), v((width, 128), BF16), v((128, width), BF16),
        v((1, width), F32), v((32, width), BF16), v(w_gate_up.shape, BF16), v((2048, width), BF16),
        v((8, rows), jnp.int32), v((n_pages, entries), BF16), v((16, 16), jnp.int32), v((16, 16), jnp.int32),
        v((128, 128), F32), v((128, 128), F32), v((64, 128), F32), v((64, 128), F32),
        v((1024, width), BF16), v((rows, width), BF16), v((n_seq, rows, 128), BF16), v((2, 2, rows, 128), BF16),
        v((rows, 128), BF16), v((rows, 128), BF16), v((2, 2, rows, 128), F32), v((2, rows, 128), BF16),
        v((2, rows, 128), BF16), v((8, rows, 128), BF16), v((rows, width), BF16), v((rows, width), BF16),
        v((rows, 128), F32), v((4, rows, 128), F32), v((rows, 2048), BF16),
        v((4, half, COLS), BF16), v((4, half, COLS), F32), v((4, half, COLS), BF16), v((4, half, COLS), BF16),
        v((8, 128), F32), v((4, 4, half // 4, COLS), BF16), v((4, rows, COLS), BF16),
        v((128, entries), BF16), v((128, entries), BF16),
    ]
    d = pltpu.SemaphoreType.DMA
    scratch += [
        d((21,)), d((n_seq,)), d((n_seq,)), d, d, d, d, d((n_seq,)), d((n_seq,)),
        d((4,)), d((8,)), d((3,)), d((4,)), d((8,)), d((3,)),
        d((4,)), d((4,)), d((4, 3)), d((4, 4)), d((4, 4)), d((4, 8)), d((4, 3)), d((5,)),
    ]
    args = (
        tokens, attn_gain.reshape(1, width), w_query, key_weight.T, value_weight.T, w_out, moe_gain.reshape(1, width),
        w_router.T, w_gate_up, w_down.reshape(2048, width), expert_ids.T, source_cache_pages.reshape(n_pages, entries),
        req_pages, req_dest, *[jnp.asarray(t) for t in tables],
    )
    any_spec = pl.BlockSpec(memory_space=pl.ANY)
    layer_out, relaid = pl.pallas_call(
        functools.partial(kernel, n_seq),
        out_shape=(
            jax.ShapeDtypeStruct((rows, width), BF16),
            jax.ShapeDtypeStruct((128, entries), BF16),
        ),
        in_specs=[any_spec] * len(args),
        out_specs=(any_spec, any_spec),
        scratch_shapes=scratch,
        compiler_params=pltpu.CompilerParams(
            collective_id=0, has_side_effects=True, vmem_limit_bytes=60 * 1024 * 1024
        ),
        name="layer",
    )(*args)
    return layer_out, relaid.reshape(128, 1, entries)


def solution(mesh):
    in_specs = (
        P("seq", None), P(), P(None, "head"), P(None, "head"), P(None, "head"), P("head", None), P(), P(),
        P("head", None, None), P("head", None, None), P("seq", None), P("seq", "head", None), P(), P(),
    )
    out_specs = (P("seq", None), P("seq", "head", None))
    return jax.shard_map(
        functools.partial(per_device, mesh.shape["seq"]),
        mesh=mesh, in_specs=in_specs, out_specs=out_specs, check_vma=False,
    )
```

```python
import functools

import jax
import jax.numpy as jnp
import numpy as np
from jax import lax
from jax.experimental import pallas as pl
from jax.experimental.pallas import tpu as pltpu
from jax.sharding import PartitionSpec as P

HD = 64
LANES = 128
COLS = 256
F32 = jnp.float32
BF16 = jnp.bfloat16
NT = (((1,), (1,)), ((), ()))


def rotary_tables(tokens, rows):
    lane_freq = np.arange(LANES) % (HD // 2)
    freq = 10000.0 ** (lane_freq * (-2.0 / HD))
    coarse = np.arange(tokens // rows)[:, None] * float(rows) * freq[None, :]
    fine = np.arange(rows)[:, None] * freq[None, :]
    table = [np.cos(coarse), np.sin(coarse), np.cos(fine), np.sin(fine)]
    return [part.astype(np.float32) for part in table]


def dot(a, b, dims=None):
    if dims is None:
        return jnp.dot(a, b, preferred_element_type=F32)
    return lax.dot_general(a, b, dims, preferred_element_type=F32)


def kernel(
    n_seq,
    tok_h, again_h, wq_h, wkt_h, wvt_h, wo_h, mgain_h, wrt_h, wgu_h, wd_h, ids_h, pages_h, rp_h, rd_h,
    cc_h, cs_h, fc_h, fs_h,
    out_h, precv,
    tok, again, wq, wkvt, mgain, wrt, wgu, wd, ids, pages, rp, rd, cc, cs, fc, fs,
    woutg, normed, kvbuf, qbuf, qpack, qrecv, acc, part, prt, ctxg, hidden, moe, gcol, gb, act,
    p1s, keep, p1r, p2s, p2r, outb, psend,
    sem_in, kv_s, kv_r, q_s, q_r, pt_s, pt_r, pg_s, pg_r, wo_s, wo_r, cx_s, cx_r,
    l1_s, l1_r, l2_s, l2_r, ag_s, ag_r, ag_f, out_sem,
):
    me = lax.axis_index("seq")
    hh = lax.axis_index("head")
    zz = hh // 2
    core = hh % 2
    mate = hh + 1 - 2 * core
    rows = tok.shape[0]
    half = rows // 2
    light = me < n_seq // 2
    last = n_seq - 1
    partner = last - me

    barrier = pltpu.get_barrier_semaphore()
    for k in range(1, n_seq):
        pl.semaphore_signal(barrier, inc=1, device_id={"seq": (me + k) % n_seq})
    for k in range(1, 8):
        pl.semaphore_signal(barrier, inc=1, device_id={"head": (hh + k) % 8})

    loads = [
        (tok_h, tok), (again_h, again), (wq_h, wq), (wkt_h, wkvt.at[pl.ds(0, HD)]),
        (wvt_h, wkvt.at[pl.ds(HD, HD)]), (cc_h, cc), (cs_h, cs), (fc_h, fc), (fs_h, fs),
        (pages_h, pages), (rp_h, rp), (rd_h, rd),
        (mgain_h, mgain), (wrt_h, wrt), (ids_h, ids),
    ]
    copies = [pltpu.make_async_copy(src, dst, sem_in.at[i]) for i, (src, dst) in enumerate(loads)]
    n0 = len(copies)
    big = [pltpu.make_async_copy(wo_h, woutg.at[pl.ds(hh * 128, 128)], sem_in.at[n0])]
    for e in range(4):
        big.append(pltpu.make_async_copy(wgu_h.at[e], wgu.at[e], sem_in.at[n0 + 1 + e]))
    big.append(pltpu.make_async_copy(wd_h, wd, sem_in.at[n0 + 5]))
    for c in copies:
        c.start()
    for c in big:
        c.start()

    for i in (0, 1):
        copies[i].wait()
    for r in range(0, rows, 128):
        x = tok[r : r + 128, :].astype(F32)
        scale = lax.rsqrt(jnp.mean(x * x, axis=1, keepdims=True) + 1e-05)
        normed[r : r + 128, :] = (x * scale * again[...]).astype(BF16)
    for i in range(2, 9):
        copies[i].wait()

    q = dot(normed[...], wq[...])
    kv = dot(normed[...], wkvt[...], NT)
    lane = lax.broadcasted_iota(jnp.int32, (64, LANES), 1)
    first = (lane % HD) < HD // 2
    low = lane < HD
    own_kv = kvbuf.at[me]
    ccb = cc[pl.ds(pl.multiple_of(me * 8, 8), 8), :]
    csb = cs[pl.ds(pl.multiple_of(me * 8, 8), 8), :]
    for g in range(rows // 64):
        ca = ccb[g : g + 1, :]
        sa = csb[g : g + 1, :]
        cosv = ca * fc[...] - sa * fs[...]
        sinv = sa * fc[...] + ca * fs[...]
        sinv = jnp.where(first, -sinv, sinv)
        sl = slice(g * 64, g * 64 + 64)
        qg = q[sl]
        kg = kv[sl]
        qsw = jnp.where(first, pltpu.roll(qg, 96, 1), pltpu.roll(qg, 32, 1))
        ksw = jnp.where(first, pltpu.roll(kg, 96, 1), pltpu.roll(kg, 32, 1))
        qr = qg * cosv + qsw * sinv
        kr = jnp.where(low, kg * cosv + ksw * sinv, kg)
        kvbuf[me, sl, :] = kr.astype(BF16)
        qpack[sl, :] = qr.astype(BF16)
        qbuf[0, 0, sl, :] = jnp.where(low, qr, 0.0).astype(BF16)
        qbuf[0, 1, sl, :] = jnp.where(low, pltpu.roll(qr, HD, 1), 0.0).astype(BF16)

    pl.semaphore_wait(barrier, n_seq - 1 + 7)

    def kv_copy(k):
        peer = (me + k) % n_seq
        needed = jnp.where(
            peer >= n_seq // 2,
            (peer - 8 <= me) & (me < peer),
            (me < peer) | (me <= 6 - peer),
        )
        return needed, pltpu.make_async_remote_copy(
            own_kv, kvbuf.at[me], kv_s.at[k], kv_r.at[me], device_id={"seq": peer}
        )

    by_distance = [k % n_seq for d in range(1, n_seq // 2) for k in (d, -d)] + [n_seq // 2]
    q_copy = pltpu.make_async_remote_copy(qpack, qrecv, q_s, q_r, device_id={"seq": partner})
    ships = me >= n_seq // 2 + 1
    helps = me <= n_seq // 2 - 2

    @pl.when(ships)
    def _():
        q_copy.start()

    for k in by_distance:
        needed, c = kv_copy(k)

        @pl.when(needed)
        def _(c=c):
            c.start()

    up = ((zz + 1) % 4) * 2 + core
    down = ((zz + 3) % 4) * 2 + core
    across = ((zz + 2) % 4) * 2 + core

    class Gather:
        def __init__(self, piece, send_sems, recv_sems):
            self.piece, self.ss, self.rs, self.started = piece, send_sems, recv_sems, []

        def copy(self, src, part, dev, k, from_ref=None):
            ref = self.piece(src, part)
            return pltpu.make_async_remote_copy(
                ref if from_ref is None else from_ref, ref, self.ss(k), self.rs(src, part), device_id={"head": dev}
            )

        def send(self, src, part, dev, from_ref=None):
            c = self.copy(src, part, dev, len(self.started), from_ref)
            c.start()
            self.started.append(c)

        def wait(self, src, part):
            self.copy(src, part, mate, 0).wait_recv()

        def begin(self, own=(None, None)):
            for part, dev in ((0, up), (1, down), (1, up), (0, down), (0, mate), (1, mate)):
                self.send(hh, part, dev, own[part])

        def relay(self):
            for src, part, nxt in ((down, 0, up), (up, 1, down), (down, 1, None), (up, 0, None)):
                self.wait(src, part)
                if nxt is not None:
                    self.send(src, part, nxt)
                self.send(src, part, mate)

        def relay_across(self):
            for part in (0, 1):
                self.wait(across, part)
                self.send(across, part, mate)

        def finish(self):
            for z in range(4):
                for part in (0, 1):
                    self.wait(((zz + z) % 4) * 2 + 1 - core, part)

    wo = Gather(
        lambda h, p: woutg.at[pl.ds(h * 128 + p * 64, 64)], lambda k: wo_s.at[k], lambda h, p: wo_r.at[h, p]
    )
    wo.begin((wo_h.at[pl.ds(0, 64)], wo_h.at[pl.ds(64, 64)]))

    for i in range(9, 12):
        copies[i].wait()
    srow = lax.broadcasted_iota(jnp.int32, (16, 16), 0)
    mine = srow == me
    own_pages = jnp.sum(jnp.where(mine, rp[...].astype(F32), 0.0), axis=0, keepdims=True)
    own_dest = jnp.sum(jnp.where(mine, rd[...].astype(F32), 0.0), axis=0, keepdims=True)
    slot = lax.broadcasted_iota(jnp.int32, (128, 16), 0)
    req = lax.broadcasted_iota(jnp.int32, (128, 16), 1).astype(F32)
    match = own_dest == (slot // 8).astype(F32)
    send_len = jnp.sum(jnp.where(match, own_pages, 0.0), axis=1, keepdims=True)
    send_req = jnp.sum(jnp.where(match, req, 0.0), axis=1, keepdims=True)
    send_start = jnp.sum(jnp.where(req < send_req, own_pages, 0.0), axis=1, keepdims=True)
    sub = (lax.broadcasted_iota(jnp.int32, (128, 64), 0) % 8).astype(F32)
    src_row = lax.broadcasted_iota(jnp.int32, (128, 64), 1).astype(F32)
    pack = jnp.where((src_row == send_start + sub) & (sub < send_len), 1.0, 0.0).astype(BF16)

    def pack_step(i, carry):
        cols = pl.ds(pl.multiple_of(i * 1024, 1024), 1024)
        psend[:, cols] = dot(pack, pages[:, cols]).astype(BF16)
        return carry

    lax.fori_loop(0, 8, pack_step, 0)
    pg_own = pltpu.make_async_copy(psend.at[pl.ds(me * 8, 8)], precv.at[pl.ds(me * 8, 8)], pg_s.at[0])
    pg_own.start()

    def pg_copy(k):
        peer = (me + k) % n_seq
        return pltpu.make_async_remote_copy(
            psend.at[pl.ds(peer * 8, 8)], precv.at[pl.ds(me * 8, 8)], pg_s.at[k], pg_r.at[me],
            device_id={"seq": peer},
        )

    def attend(w, h, r0, nr, kblk, v1, diag):
        qt = qbuf[w, h, r0 : r0 + nr, :]
        s = dot(qt, kblk, NT)
        wts = jnp.exp(30.0 * jnp.tanh(s * (1.0 / 240.0)))
        if diag:
            tri = lax.broadcasted_iota(jnp.int32, s.shape, 1) <= lax.broadcasted_iota(jnp.int32, s.shape, 0)
            wts = jnp.where(tri, wts, 0.0)
        return dot(wts.astype(BF16), v1)

    def ones_in(kv_part):
        keep_low = lax.broadcasted_iota(jnp.int32, kv_part.shape, 1) < HD
        return jnp.where(keep_low, jnp.ones_like(kv_part), kv_part)

    ka, kb = kvbuf[me, :half, :], kvbuf[me, half:, :]
    va, vb = ones_in(ka), ones_in(kb)
    for h in range(2):
        acc[0, h, :half, :] = attend(0, h, 0, half, ka, va, True)
        acc[0, h, half:, :] = attend(0, h, half, half, ka, va, False) + attend(0, h, half, half, kb, vb, True)
    acc[1] = jnp.zeros_like(acc[1])

    def block(w, b):
        kblk = kvbuf[b]
        v1 = ones_in(kblk)
        for h in range(2):
            for r0 in (0, half):
                acc[w, h, r0 : r0 + half, :] += attend(w, h, r0, half, kblk, v1, False)

    def kv_wait(b):
        pltpu.make_async_remote_copy(
            own_kv, kvbuf.at[b], kv_s.at[0], kv_r.at[b], device_id={"seq": partner}
        ).wait_recv()

    p_copy = pltpu.make_async_remote_copy(part, prt, pt_s, pt_r, device_id={"seq": partner})

    @pl.when(helps)
    def _():
        q_copy.wait_recv()
        qr = qrecv[...]
        low_q = lax.broadcasted_iota(jnp.int32, qr.shape, 1) < HD
        zero = jnp.zeros_like(qr)
        qbuf[1, 0] = jnp.where(low_q, qr, zero)
        qbuf[1, 1] = jnp.where(low_q, pltpu.roll(qr.astype(F32), HD, 1).astype(BF16), zero)

        def help_step(b, carry):
            @pl.when(b != me)
            def _():
                kv_wait(b)

            block(1, b)
            return carry

        lax.fori_loop(0, 7 - me, help_step, 0)
        part[...] = acc[1].astype(BF16)
        p_copy.start()


    def own_step(i, carry):
        b = me - 1 - i

        @pl.when(jnp.logical_not(light) | (b > 6 - me))
        def _():
            kv_wait(b)

        block(0, b)
        return carry

    n_own = jnp.where(light, me, 8)
    lax.fori_loop(0, n_own // 2, own_step, 0)
    wo.relay()
    lax.fori_loop(n_own // 2, n_own, own_step, 0)
    wo.relay_across()

    for k in by_distance:
        pg_copy(k).start()

    @pl.when(ships)
    def _():
        p_copy.wait_recv()
        acc[0] = acc[0] + prt[...].astype(F32)

    low_c = lax.broadcasted_iota(jnp.int32, (rows, LANES), 1) < HD
    c0 = acc[0, 0] / pltpu.roll(acc[0, 0], HD, 1)
    c1 = acc[0, 1] / pltpu.roll(acc[0, 1], HD, 1)
    ctxg[hh] = jnp.where(low_c, pltpu.roll(c0, HD, 1), c1).astype(BF16)

    cx = Gather(lambda h, p: ctxg.at[h, pl.ds(p * half, half)], lambda k: cx_s.at[k], lambda h, p: cx_r.at[h, p])
    cx.begin()
    big[0].wait()
    for i in range(12, 15):
        copies[i].wait()
    cx.relay()
    cx.relay_across()
    wo.finish()
    cx.finish()

    for r in (0, half):
        x = jnp.concatenate([ctxg[i, r : r + half, :] for i in range(8)], axis=1)
        hid = (tok[r : r + half, :].astype(F32) + dot(x, woutg[...])).astype(BF16)
        hidden[r : r + half, :] = hid
        hf = hid.astype(F32)
        scale = lax.rsqrt(jnp.mean(hf * hf, axis=1, keepdims=True) + 1e-05)
        moe[r : r + half, :] = (hf * scale * mgain[...]).astype(BF16)

    logits = dot(wrt[...], moe[...], NT)
    expert = lax.broadcasted_iota(jnp.int32, logits.shape, 0)
    chosen = expert == ids[0:1, :]
    for k in range(1, 8):
        chosen = chosen | (expert == ids[k : k + 1, :])
    raised = jnp.where(chosen, jnp.exp(logits), 0.0)
    gates = raised / jnp.sum(raised, axis=0, keepdims=True)
    gcol[...] = jnp.transpose(jnp.concatenate([gates, jnp.zeros((96, rows), F32)], axis=0))
    lane_r = lax.broadcasted_iota(jnp.int32, (rows, LANES), 1)
    for e in range(4):
        picked = jnp.sum(jnp.where(lane_r == hh * 4 + e, gcol[...], 0.0), axis=1, keepdims=True)
        gb[e] = jnp.broadcast_to(picked, (rows, LANES))

    for e in range(1, 6):
        big[e].wait()

    def expert_step(e, carry):
        gate2 = jnp.concatenate([gb[e], gb[e]], axis=1)
        for c in range(2):
            g = dot(moe[...], wgu[e, :, c * COLS : c * COLS + COLS])
            u = dot(moe[...], wgu[e, :, 512 + c * COLS : 512 + c * COLS + COLS])
            a = g / (1.0 + jnp.exp(-g)) * u * gate2
            act[:, pl.ds(pl.multiple_of(e * 512 + c * COLS, COLS), COLS)] = a.astype(BF16)
        return carry

    lax.fori_loop(0, 4, expert_step, 0)

    own_half = pl.ds(pl.multiple_of(core * half, half), half)
    mate_half = pl.ds(pl.multiple_of((1 - core) * half, half), half)
    quarter = half // 4
    own_rows = pl.ds(pl.multiple_of(core * half + zz * quarter, quarter), quarter)
    ring = [(across, (zz + 2) % 4), (up, (zz + 1) % 4), (down, (zz + 3) % 4)]

    def l1_copy(n):
        return pltpu.make_async_remote_copy(p1s.at[n], p1r.at[n], l1_s.at[n], l1_r.at[n], device_id={"head": mate})

    def l2_copy(n, i):
        dev, z = ring[i]
        return pltpu.make_async_remote_copy(
            p2s.at[n, pl.ds(z * quarter, quarter)], p2r.at[n, i], l2_s.at[n, i], l2_r.at[n, i],
            device_id={"head": dev},
        )

    def ag_copy(n, h, dev, ss):
        at = outb.at[n, pl.ds((h % 2) * half + (h // 2) * quarter, quarter)]
        return pltpu.make_async_remote_copy(at, at, ss, ag_r.at[n, h], device_id={"head": dev})

    def out_copy(n):
        return pltpu.make_async_copy(outb.at[n], out_h.at[:, pl.ds(n * COLS, COLS)], out_sem.at[n])

    def stage_down(n):
        wcol = wd[:, n * COLS : n * COLS + COLS]
        p1s[n] = dot(act[mate_half, :], wcol).astype(BF16)
        l1_copy(n).start()
        keep[n] = dot(act[own_half, :], wcol)

    def stage_sum(n):
        l1_copy(n).wait_recv()
        t = keep[n] + p1r[n].astype(F32)
        p2s[n] = t.astype(BF16)
        for i in range(3):
            l2_copy(n, i).start()
        keep[n] = t

    def stage_final(n):
        t = keep[n, pl.ds(pl.multiple_of(zz * quarter, quarter), quarter), :]
        t = t + hidden[own_rows, n * COLS : n * COLS + COLS].astype(F32)
        for i in (1, 2, 0):
            l2_copy(n, i).wait_recv()
            t = t + p2r[n, i].astype(F32)
        outb[n, own_rows, :] = t.astype(BF16)
        for i in range(3):
            ag_copy(n, hh, ring[i][0], ag_s.at[n, i]).start()
        ag_copy(n, hh, mate, ag_f.at[n, 3]).start()

    def stage_pass(n):
        for i in (1, 2, 0):
            ag_copy(n, ring[i][0], mate, ag_s.at[n, i]).wait_recv()
            ag_copy(n, ring[i][0], mate, ag_f.at[n, i]).start()

    def stage_out(n):
        for z in range(4):
            ag_copy(n, ((zz + z) % 4) * 2 + 1 - core, mate, ag_s.at[n, 0]).wait_recv()
        out_copy(n).start()

    steps = {"d": stage_down, "s": stage_sum, "f": stage_final, "p": stage_pass, "o": stage_out}
    for step in "d0 d1 s0 d2 s1 d3 s2 s3 f0 f1 f2 f3 p0 p1 o0 p2 o1 p3 o2 o3".split():
        steps[step[0]](int(step[1]))

    pg_own.wait()
    for k in by_distance:
        src = (me + k) % n_seq
        pltpu.make_async_remote_copy(
            psend.at[pl.ds(0, 8)], precv.at[pl.ds(src * 8, 8)], pg_s.at[k], pg_r.at[src], device_id={"seq": src}
        ).wait_recv()
    for k in by_distance:
        pg_copy(k).wait_send()

    for k in range(1, n_seq):
        needed, c = kv_copy(k)

        @pl.when(needed)
        def _(c=c):
            c.wait_send()

    @pl.when(ships)
    def _():
        q_copy.wait_send()

    @pl.when(helps)
    def _():
        p_copy.wait_send()

    for c in wo.started + cx.started:
        c.wait_send()
    for n in range(4):
        l1_copy(n).wait_send()
        for i in range(3):
            l2_copy(n, i).wait_send()
            ag_copy(n, hh, ring[i][0], ag_s.at[n, i]).wait_send()
            ag_copy(n, ring[i][0], mate, ag_f.at[n, i]).wait_send()
        ag_copy(n, hh, mate, ag_f.at[n, 3]).wait_send()
        out_copy(n).wait()


def finish_kernel(n_seq, sum_h, pages_h, rp_h, rd_h, out_h, relaid_h, rows_v, got, placed, rp, rd, in_sem, out_sem):
    me = lax.axis_index("seq")
    n_col = 8
    width = got.shape[1] // n_col
    tall = rows_v.shape[0] // 4
    tables = [pltpu.make_async_copy(rp_h, rp, in_sem.at[12]), pltpu.make_async_copy(rd_h, rd, in_sem.at[13])]
    for c in tables:
        c.start()

    def load(i):
        cols = pl.ds(i * width, width)
        return pltpu.make_async_copy(pages_h.at[:, cols], got.at[:, cols], in_sem.at[i])

    def store(i):
        cols = pl.ds(i * width, width)
        return pltpu.make_async_copy(placed.at[:, cols], relaid_h.at[:, cols], out_sem.at[i])

    def load_rows(i):
        at = pl.ds(i * tall, tall)
        return pltpu.make_async_copy(sum_h.at[at], rows_v.at[at], in_sem.at[n_col + i])

    def store_rows(i):
        at = pl.ds(i * tall, tall)
        return pltpu.make_async_copy(rows_v.at[at], out_h.at[at], out_sem.at[n_col + i])

    for i in range(n_col):
        load(i).start()
    for i in range(4):
        load_rows(i).start()
    for c in tables:
        c.wait()
    len_m = jnp.sum(jnp.where(rd[...] == me, rp[...].astype(F32), 0.0), axis=1, keepdims=True)
    s_of = lax.broadcasted_iota(jnp.int32, (16, 128), 1) // 8
    s_row = lax.broadcasted_iota(jnp.int32, (16, 128), 0)
    len_c = jnp.sum(jnp.where(s_row == s_of, len_m, 0.0), axis=0, keepdims=True)
    off_c = jnp.sum(jnp.where(s_row < s_of, len_m, 0.0), axis=0, keepdims=True)
    to_row = lax.broadcasted_iota(jnp.int32, (128, 128), 0).astype(F32)
    sub_c = (lax.broadcasted_iota(jnp.int32, (128, 128), 1) % 8).astype(F32)
    place = jnp.where((to_row == off_c + sub_c) & (sub_c < len_c), 1.0, 0.0).astype(BF16)
    for i in range(n_col):
        load(i).wait()
        cols = slice(i * width, (i + 1) * width)
        placed[:, cols] = dot(place, got[:, cols]).astype(BF16)
        store(i).start()
    for i in range(4):
        load_rows(i).wait()
        store_rows(i).start()
    for i in range(n_col):
        store(i).wait()
    for i in range(4):
        store_rows(i).wait()


def per_device(
    n_seq, tokens, attn_gain, w_query, key_weight, value_weight, w_out, moe_gain, w_router, w_gate_up, w_down,
    expert_ids, source_cache_pages, req_pages, req_dest,
):
    rows, width = tokens.shape
    n_pages, _, entries = source_cache_pages.shape
    tables = rotary_tables(rows * n_seq, 64)
    half = rows // 2
    v = pltpu.VMEM
    scratch = [
        v((rows, width), BF16), v((1, width), F32), v((width, 128), BF16), v((128, width), BF16),
        v((1, width), F32), v((32, width), BF16), v(w_gate_up.shape, BF16), v((2048, width), BF16),
        v((8, rows), jnp.int32), v((n_pages, entries), BF16), v((16, 16), jnp.int32), v((16, 16), jnp.int32),
        v((128, 128), F32), v((128, 128), F32), v((64, 128), F32), v((64, 128), F32),
        v((1024, width), BF16), v((rows, width), BF16), v((n_seq, rows, 128), BF16), v((2, 2, rows, 128), BF16),
        v((rows, 128), BF16), v((rows, 128), BF16), v((2, 2, rows, 128), F32), v((2, rows, 128), BF16),
        v((2, rows, 128), BF16), v((8, rows, 128), BF16), v((rows, width), BF16), v((rows, width), BF16),
        v((rows, 128), F32), v((4, rows, 128), F32), v((rows, 2048), BF16),
        v((4, half, COLS), BF16), v((4, half, COLS), F32), v((4, half, COLS), BF16), v((4, half, COLS), BF16),
        v((4, 3, half // 4, COLS), BF16),
        v((4, rows, COLS), BF16), v((128, entries), BF16),
    ]
    d = pltpu.SemaphoreType.DMA
    scratch += [
        d((21,)), d((n_seq,)), d((n_seq,)), d, d, d, d, d((n_seq,)), d((n_seq,)),
        d((14,)), d((8, 2)), d((14,)), d((8, 2)),
        d((4,)), d((4,)), d((4, 3)), d((4, 3)), d((4, 3)), d((4, 8)), d((4, 4)), d((4,)),
    ]
    args = (
        tokens, attn_gain.reshape(1, width), w_query, key_weight.T, value_weight.T, w_out, moe_gain.reshape(1, width),
        w_router.T, w_gate_up, w_down.reshape(2048, width), expert_ids.T, source_cache_pages.reshape(n_pages, entries),
        req_pages, req_dest, *[jnp.asarray(t) for t in tables],
    )
    any_spec = pl.BlockSpec(memory_space=pl.ANY)
    shapes = (jax.ShapeDtypeStruct((rows, width), BF16), jax.ShapeDtypeStruct((128, entries), BF16))
    summed, received = pl.pallas_call(
        functools.partial(kernel, n_seq),
        out_shape=shapes,
        in_specs=[any_spec] * len(args),
        out_specs=(any_spec, any_spec),
        scratch_shapes=scratch,
        compiler_params=pltpu.CompilerParams(
            collective_id=0, has_side_effects=True, vmem_limit_bytes=60 * 1024 * 1024
        ),
        name="layer",
    )(*args)
    layer_out, relaid = pl.pallas_call(
        functools.partial(finish_kernel, n_seq),
        out_shape=shapes,
        in_specs=[any_spec] * 4,
        out_specs=(any_spec, any_spec),
        scratch_shapes=[
            v((rows, width), BF16), v((128, entries), BF16), v((128, entries), BF16),
            v((16, 16), jnp.int32), v((16, 16), jnp.int32), d((14,)), d((12,)),
        ],
        compiler_params=pltpu.CompilerParams(vmem_limit_bytes=60 * 1024 * 1024),
        name="finish",
    )(summed, received, req_pages, req_dest)
    return layer_out, relaid.reshape(128, 1, entries)


def solution(mesh):
    in_specs = (
        P("seq", None), P(), P(None, "head"), P(None, "head"), P(None, "head"), P("head", None), P(), P(),
        P("head", None, None), P("head", None, None), P("seq", None), P("seq", "head", None), P(), P(),
    )
    out_specs = (P("seq", None), P("seq", "head", None))
    return jax.shard_map(
        functools.partial(per_device, mesh.shape["seq"]),
        mesh=mesh, in_specs=in_specs, out_specs=out_specs, check_vma=False,
    )
```

```python
import functools

import jax
import jax.numpy as jnp
import numpy as np
from jax import lax
from jax.experimental import pallas as pl
from jax.experimental.pallas import tpu as pltpu
from jax.sharding import PartitionSpec as P

HD = 64
LANES = 128
COLS = 256
F32 = jnp.float32
BF16 = jnp.bfloat16
NT = (((1,), (1,)), ((), ()))

TASKS = (
    (),
    ((0, 0),),
    ((1, 1), (1, 2), (0, 1), (1, 3), (1, 6), (1, 0), (1, 5), (0, 0), (1, 4),),
    ((1, 0), (1, 3), (1, 7), (1, 1), (0, 0), (0, 1), (0, 2), (1, 4),),
    ((1, 0), (1, 3), (0, 0), (1, 7), (1, 8), (0, 3), (1, 1), (0, 1), (1, 2), (0, 2),),
    ((1, 1), (1, 2), (1, 5), (0, 1), (1, 4), (1, 6), (0, 2), (0, 4), (0, 3), (0, 0),),
    ((1, 5), (1, 3), (0, 3), (0, 2), (1, 0), (0, 0),),
    ((1, 6), (0, 6), (1, 2), (1, 5), (0, 2), (1, 8), (0, 4), (1, 1), (0, 1),),
    ((1, 4), (1, 8), (1, 11), (1, 12), (1, 9), (1, 7), (0, 7), (1, 0), (0, 0), (0, 3),),
    ((1, 5), (0, 5), (1, 4), (0, 4), (1, 1), (0, 6),),
    ((0, 9), (0, 6), (0, 5), (0, 8), (0, 2),),
    ((0, 10), (0, 9), (0, 7), (0, 3), (0, 4), (0, 0),),
    ((1, 12), (1, 0), (1, 8), (0, 0), (1, 4), (0, 11), (0, 4), (0, 9), (1, 1), (0, 1), (0, 7), (0, 5),),
    ((1, 10), (1, 8), (0, 10), (1, 2), (1, 3), (0, 2), (0, 3), (1, 6), (0, 5), (0, 1), (0, 6),),
    ((0, 13), (0, 10), (0, 9), (0, 11), (0, 3), (0, 2), (0, 6), (0, 7), (0, 5),),
    ((0, 11), (0, 12), (0, 14), (0, 13), (0, 8), (0, 10), (0, 7), (0, 9),),
)
SENDS = (
    (3, 4, 12, 2, 8, 1, 6, 5, 11,),
    (2, 5, 3, 4, 9, 12, 13, 7,),
    (5, 7, 13, 3, 6, 14, 4, 10,),
    (2, 4, 6, 13, 11, 14, 5, 8,),
    (5, 8, 9, 12, 3, 7, 2, 11,),
    (6, 9, 7, 2, 10, 13, 12, 14,),
    (7, 2, 5, 10, 13, 9, 14,),
    (3, 4, 8, 11, 15, 12, 14,),
    (12, 4, 13, 7, 10, 15,),
    (8, 10, 11, 12, 14, 15,),
    (13, 11, 14, 15,),
    (8, 15, 12, 14,),
    (8, 15,),
    (14, 15,),
    (15,),
    (),
)
HELPER = (-1, -1, -1, -1, -1, -1, 9, 6, 5, 4, 3, 7, 13, 8, 12, 2)


def pack_words(lists, per_word, bits):
    words = -(-max(len(x) for x in lists) // per_word)
    return [
        [sum(code << bits * k for k, code in enumerate(x[w * per_word : (w + 1) * per_word])) for x in lists]
        for w in range(words)
    ]


def task_codes(d):
    seen, codes = {d}, []
    for w, b in TASKS[d]:
        codes.append((b not in seen) * 32 + w * 16 + b)
        seen.add(b)
    return codes


def rotary_tables(tokens, rows):
    lane_freq = np.arange(LANES) % (HD // 2)
    freq = 10000.0 ** (lane_freq * (-2.0 / HD))
    coarse = np.arange(tokens // rows)[:, None] * float(rows) * freq[None, :]
    fine = np.arange(rows)[:, None] * freq[None, :]
    table = [np.cos(coarse), np.sin(coarse), np.cos(fine), np.sin(fine)]
    return [part.astype(np.float32) for part in table]


def dot(a, b, dims=None):
    if dims is None:
        return jnp.dot(a, b, preferred_element_type=F32)
    return lax.dot_general(a, b, dims, preferred_element_type=F32)


def kernel(
    n_seq,
    tok_h, again_h, wq_h, wkt_h, wvt_h, wo_h, mgain_h, wrt_h, wgu_h, wd_h, ids_h, pages_h, rp_h, rd_h,
    cc_h, cs_h, fc_h, fs_h,
    out_h, precv,
    tok, again, wq, wkvt, mgain, wrt, wgu, wd, ids, pages, rp, rd, cc, cs, fc, fs,
    woutg, normed, kvbuf, qbuf, qpack, qrecv, acc, partn, partd, prtn, prtd, ctxg, hidden, moe, down_out, gb, act,
    p1s, keep, p1r, p2s, p2r, outb, psend,
    sem_in, kv_s, kv_r, q_s, q_r, pt_s, pt_r, pg_s, pg_r, wo_s, wo_r, cx_s, cx_r,
    l1_s, l1_r, l2_s, l2_r, ag_s, ag_r, ag_f, out_sem,
):
    me = lax.axis_index("seq")
    hh = lax.axis_index("head")
    zz = hh // 2
    core = hh % 2
    mate = hh + 1 - 2 * core
    rows = tok.shape[0]
    half = rows // 2

    def pick(values):
        out = values[0]
        for i in range(1, n_seq):
            out = jnp.where(me == i, values[i], out)
        return out

    helps_whom = [HELPER.index(d) if d in HELPER else -1 for d in range(n_seq)]
    my_helper, my_guest = pick(HELPER), pick(helps_whom)
    ships, helps = my_helper >= 0, my_guest >= 0
    n_tasks = pick([len(t) for t in TASKS])
    n_sends = pick([len(t) for t in SENDS])
    task_words = [pick(w) for w in pack_words([task_codes(d) for d in range(n_seq)], 5, 6)]
    send_words = [pick(w) for w in pack_words(SENDS, 7, 4)]
    max_sends = max(len(t) for t in SENDS)
    guest_steps = [[i for i, t in enumerate(TASKS[d]) if t[0] == 1] or [-1] for d in range(n_seq)]
    first_guest, last_guest = pick([g[0] for g in guest_steps]), pick([g[-1] for g in guest_steps])

    barrier = pltpu.get_barrier_semaphore()
    for k in range(1, n_seq):
        pl.semaphore_signal(barrier, inc=1, device_id={"seq": (me + k) % n_seq})
    for k in range(1, 8):
        pl.semaphore_signal(barrier, inc=1, device_id={"head": (hh + k) % 8})

    loads = [
        (tok_h, tok), (again_h, again), (wq_h, wq), (wkt_h, wkvt.at[pl.ds(0, HD)]),
        (wvt_h, wkvt.at[pl.ds(HD, HD)]), (cc_h, cc), (cs_h, cs), (fc_h, fc), (fs_h, fs),
        (pages_h, pages), (rp_h, rp), (rd_h, rd),
        (mgain_h, mgain), (wrt_h, wrt), (ids_h, ids),
    ]
    copies = [pltpu.make_async_copy(src, dst, sem_in.at[i]) for i, (src, dst) in enumerate(loads)]
    n0 = len(copies)
    big = [pltpu.make_async_copy(wo_h, woutg.at[pl.ds(hh * 128, 128)], sem_in.at[n0])]
    for e in range(4):
        big.append(pltpu.make_async_copy(wgu_h.at[e], wgu.at[e], sem_in.at[n0 + 1 + e]))
    big.append(pltpu.make_async_copy(wd_h, wd, sem_in.at[n0 + 5]))
    for c in copies:
        c.start()
    for c in big:
        c.start()

    for i in (0, 1):
        copies[i].wait()
    for r in range(0, rows, 128):
        x = tok[r : r + 128, :].astype(F32)
        scale = lax.rsqrt(jnp.mean(x * x, axis=1, keepdims=True) + 1e-05)
        normed[r : r + 128, :] = (x * scale * again[...]).astype(BF16)
    for i in range(2, 9):
        copies[i].wait()

    q = dot(normed[...], wq[...])
    kv = dot(normed[...], wkvt[...], NT)
    lane = lax.broadcasted_iota(jnp.int32, (64, LANES), 1)
    first = (lane % HD) < HD // 2
    low = lane < HD
    own_kv = kvbuf.at[me]
    ccb = cc[pl.ds(pl.multiple_of(me * 8, 8), 8), :]
    csb = cs[pl.ds(pl.multiple_of(me * 8, 8), 8), :]
    for g in range(rows // 64):
        ca = ccb[g : g + 1, :]
        sa = csb[g : g + 1, :]
        cosv = ca * fc[...] - sa * fs[...]
        sinv = sa * fc[...] + ca * fs[...]
        sinv = jnp.where(first, -sinv, sinv)
        sl = slice(g * 64, g * 64 + 64)
        qg = q[sl]
        kg = kv[sl]
        qsw = jnp.where(first, pltpu.roll(qg, 96, 1), pltpu.roll(qg, 32, 1))
        ksw = jnp.where(first, pltpu.roll(kg, 96, 1), pltpu.roll(kg, 32, 1))
        qr = qg * cosv + qsw * sinv
        kr = jnp.where(low, kg * cosv + ksw * sinv, kg)
        kvbuf[me, sl, :] = kr.astype(BF16)
        qpack[sl, :] = qr.astype(BF16)
        qbuf[0, 0, sl, :] = jnp.where(low, qr, 0.0).astype(BF16)
        qbuf[0, 1, sl, :] = jnp.where(low, pltpu.roll(qr, HD, 1), 0.0).astype(BF16)

    pl.semaphore_wait(barrier, n_seq - 1 + 7)

    def kv_copy(i):
        peer = (send_words[i // 7] // 16 ** (i % 7)) % 16
        return i < n_sends, pltpu.make_async_remote_copy(
            own_kv, kvbuf.at[me], kv_s.at[i], kv_r.at[me], device_id={"seq": peer}
        )

    def torus_peer(k):
        return ((me // 4 + k // 4) % 4) * 4 + (me % 4 + k % 4) % 4

    by_distance = sorted(range(1, n_seq), key=lambda k: (min(k // 4, 4 - k // 4) + min(k % 4, 4 - k % 4), k))
    q_copy = pltpu.make_async_remote_copy(qpack, qrecv, q_s, q_r, device_id={"seq": my_helper})

    @pl.when(ships)
    def _():
        q_copy.start()

    for i in range(max_sends):
        needed, c = kv_copy(i)

        @pl.when(needed)
        def _(c=c):
            c.start()

    up = ((zz + 1) % 4) * 2 + core
    down = ((zz + 3) % 4) * 2 + core
    across = ((zz + 2) % 4) * 2 + core

    class Gather:
        def __init__(self, piece, send_sems, recv_sems):
            self.piece, self.ss, self.rs, self.started = piece, send_sems, recv_sems, []

        def copy(self, src, part, dev, k, from_ref=None):
            ref = self.piece(src, part)
            return pltpu.make_async_remote_copy(
                ref if from_ref is None else from_ref, ref, self.ss(k), self.rs(src, part), device_id={"head": dev}
            )

        def send(self, src, part, dev, from_ref=None):
            c = self.copy(src, part, dev, len(self.started), from_ref)
            c.start()
            self.started.append(c)

        def wait(self, src, part):
            self.copy(src, part, mate, 0).wait_recv()

        def begin(self, own=(None, None)):
            for part, dev in ((0, up), (1, down), (1, up), (0, down), (0, mate), (1, mate)):
                self.send(hh, part, dev, own[part])

        def relay(self):
            for src, part, nxt in ((down, 0, up), (up, 1, down), (down, 1, None), (up, 0, None)):
                self.wait(src, part)
                if nxt is not None:
                    self.send(src, part, nxt)
                self.send(src, part, mate)

        def relay_across(self):
            for part in (0, 1):
                self.wait(across, part)
                self.send(across, part, mate)

        def finish(self):
            for z in range(4):
                for part in (0, 1):
                    self.wait(((zz + z) % 4) * 2 + 1 - core, part)

    wo = Gather(
        lambda h, p: woutg.at[pl.ds(h * 128 + p * 64, 64)], lambda k: wo_s.at[k], lambda h, p: wo_r.at[h, p]
    )
    wo.begin((wo_h.at[pl.ds(0, 64)], wo_h.at[pl.ds(64, 64)]))

    for i in range(9, 12):
        copies[i].wait()
    srow = lax.broadcasted_iota(jnp.int32, (16, 16), 0)
    mine = srow == me
    own_pages = jnp.sum(jnp.where(mine, rp[...].astype(F32), 0.0), axis=0, keepdims=True)
    own_dest = jnp.sum(jnp.where(mine, rd[...].astype(F32), 0.0), axis=0, keepdims=True)
    slot = lax.broadcasted_iota(jnp.int32, (128, 16), 0)
    req = lax.broadcasted_iota(jnp.int32, (128, 16), 1).astype(F32)
    match = own_dest == (slot // 8).astype(F32)
    send_len = jnp.sum(jnp.where(match, own_pages, 0.0), axis=1, keepdims=True)
    send_req = jnp.sum(jnp.where(match, req, 0.0), axis=1, keepdims=True)
    send_start = jnp.sum(jnp.where(req < send_req, own_pages, 0.0), axis=1, keepdims=True)
    sub = (lax.broadcasted_iota(jnp.int32, (128, 64), 0) % 8).astype(F32)
    src_row = lax.broadcasted_iota(jnp.int32, (128, 64), 1).astype(F32)
    pack = jnp.where((src_row == send_start + sub) & (sub < send_len), 1.0, 0.0).astype(BF16)

    def pack_step(i, carry):
        cols = pl.ds(pl.multiple_of(i * 1024, 1024), 1024)
        psend[:, cols] = dot(pack, pages[:, cols]).astype(BF16)
        return carry

    lax.fori_loop(0, 8, pack_step, 0)
    pg_own = pltpu.make_async_copy(psend.at[pl.ds(me * 8, 8)], precv.at[pl.ds(me * 8, 8)], pg_s.at[0])
    pg_own.start()

    def pg_copy(k):
        peer = torus_peer(k)
        return pltpu.make_async_remote_copy(
            psend.at[pl.ds(peer * 8, 8)], precv.at[pl.ds(me * 8, 8)], pg_s.at[k], pg_r.at[me],
            device_id={"seq": peer},
        )

    def attend(w, h, r0, nr, kblk, v1, diag):
        qt = qbuf[w, h, r0 : r0 + nr, :]
        s = dot(qt, kblk, NT)
        wts = jnp.exp(30.0 * jnp.tanh(s * (1.0 / 240.0)))
        if diag:
            tri = lax.broadcasted_iota(jnp.int32, s.shape, 1) <= lax.broadcasted_iota(jnp.int32, s.shape, 0)
            wts = jnp.where(tri, wts, 0.0)
        return dot(wts.astype(BF16), v1)

    def ones_in(kv_part):
        keep_low = lax.broadcasted_iota(jnp.int32, kv_part.shape, 1) < HD
        return jnp.where(keep_low, jnp.ones_like(kv_part), kv_part)

    ka, kb = kvbuf[me, :half, :], kvbuf[me, half:, :]
    va, vb = ones_in(ka), ones_in(kb)
    for h in range(2):
        acc[0, h, :half, :] = attend(0, h, 0, half, ka, va, True)
        acc[0, h, half:, :] = attend(0, h, half, half, ka, va, False) + attend(0, h, half, half, kb, vb, True)
    acc[1] = jnp.zeros_like(acc[1])

    def block(w, b):
        kblk = kvbuf[b]
        v1 = ones_in(kblk)
        tiles = [(h, k0) for h in range(2) for k0 in (0, half)]

        def scores(h, k0):
            return dot(qbuf[w, h], kblk[k0 : k0 + half], NT)

        ahead = scores(*tiles[0])
        for i, (h, k0) in enumerate(tiles):
            s, ahead = ahead, scores(*tiles[i + 1]) if i + 1 < len(tiles) else None
            wts = jnp.exp(30.0 * jnp.tanh(s * (1.0 / 240.0)))
            acc[w, h] += dot(wts.astype(BF16), v1[k0 : k0 + half])

    def kv_wait(b):
        pltpu.make_async_remote_copy(
            own_kv, kvbuf.at[b], kv_s.at[0], kv_r.at[b], device_id={"seq": my_helper}
        ).wait_recv()

    part_copies = [
        pltpu.make_async_remote_copy(src, dst, pt_s.at[i], pt_r.at[i], device_id={"seq": my_guest})
        for i, (src, dst) in enumerate(((partn, prtn), (partd, prtd)))
    ]
    low_c = lax.broadcasted_iota(jnp.int32, (rows, LANES), 1) < HD

    def task_step(i, carry):
        word = task_words[0]
        for w in range(1, len(task_words)):
            word = jnp.where(i >= 5 * w, task_words[w], word)
        code = lax.shift_right_logical(word, 6 * (i % 5)) % 64
        b = code % 16

        @pl.when(code >= 32)
        def _():
            kv_wait(b)

        @pl.when(i == first_guest)
        def _():
            q_copy.wait_recv()
            qr = qrecv[...]
            zero = jnp.zeros_like(qr)
            qbuf[1, 0] = jnp.where(low_c, qr, zero)
            qbuf[1, 1] = jnp.where(low_c, pltpu.roll(qr.astype(F32), HD, 1).astype(BF16), zero)

        block((code // 16) % 2, b)

        @pl.when(i == last_guest)
        def _():
            partn[...] = jnp.where(low_c, pltpu.roll(acc[1, 0], HD, 1), acc[1, 1]).astype(BF16)
            for h in range(2):
                partd[h] = jnp.transpose(acc[1, h])[0:8, :]
            for c in part_copies:
                c.start()

        return carry

    lax.fori_loop(0, n_tasks // 2, task_step, 0)
    wo.relay()
    lax.fori_loop(n_tasks // 2, n_tasks, task_step, 0)
    wo.relay_across()
    early = pick([d in (2, 3, 7, 10, 11, 12, 13, 14, 15) for d in range(n_seq)])

    @pl.when(early)
    def _():
        for k in by_distance:
            pg_copy(k).start()

    acc[1, 0] = jnp.where(low_c, pltpu.roll(acc[0, 0], HD, 1), acc[0, 1])
    acc[1, 1] = jnp.where(low_c, acc[0, 0], pltpu.roll(acc[0, 1], HD, 1))

    @pl.when(ships)
    def _():
        for c in part_copies:
            c.wait_recv()
        acc[1, 0] += prtn[...].astype(F32)
        den = [jnp.transpose(jnp.broadcast_to(prtd[h, 0:1, :], (LANES, rows))) for h in range(2)]
        acc[1, 1] += jnp.where(low_c, den[0], den[1])

    ctxg[hh] = (acc[1, 0] / acc[1, 1]).astype(BF16)

    cx = Gather(lambda h, p: ctxg.at[h, pl.ds(p * half, half)], lambda k: cx_s.at[k], lambda h, p: cx_r.at[h, p])
    for part in (0, 1):
        for dev in (across, up, down, mate):
            cx.send(hh, part, dev)
    big[0].wait()
    for i in range(12, 15):
        copies[i].wait()

    def cx_pass(part):
        for src in (up, down, across):
            cx.wait(src, part)
            cx.send(src, part, mate)

    def cx_finish(part):
        for z in range(4):
            cx.wait(((zz + z) % 4) * 2 + 1 - core, part)

    wo.finish()
    cx_pass(0)
    cx_finish(0)

    def project(r):
        at = slice(r * half, r * half + half)
        x = jnp.concatenate([ctxg[i, at, :] for i in range(8)], axis=1)
        hid = (tok[at, :].astype(F32) + dot(x, woutg[...])).astype(BF16)
        hidden[at, :] = hid
        hf = hid.astype(F32)
        scale = lax.rsqrt(jnp.mean(hf * hf, axis=1, keepdims=True) + 1e-05)
        moe[at, :] = (hf * scale * mgain[...]).astype(BF16)
        logits = dot(wrt[...], moe[at, :], NT)
        expert = lax.broadcasted_iota(jnp.int32, logits.shape, 0)
        chosen = expert == ids[0:1, at]
        for k in range(1, 8):
            chosen = chosen | (expert == ids[k : k + 1, at])
        raised = jnp.where(chosen, jnp.exp(logits), 0.0)
        gates = raised / jnp.sum(raised, axis=0, keepdims=True)
        gcol = jnp.transpose(jnp.concatenate([gates, jnp.zeros((96, half), F32)], axis=0))
        lane_r = lax.broadcasted_iota(jnp.int32, (half, LANES), 1)
        for e in range(4):
            picked = jnp.sum(jnp.where(lane_r == hh * 4 + e, gcol, 0.0), axis=1, keepdims=True)
            gb[e, at, :] = jnp.broadcast_to(picked, (half, LANES))

    def experts(r, first, stop):
        at = slice(r * half, r * half + half)

        def expert_step(e, carry):
            gate2 = jnp.concatenate([gb[e, at, :], gb[e, at, :]], axis=1)
            for c in range(2):
                g = dot(moe[at, :], wgu[e, :, c * COLS : c * COLS + COLS])
                u = dot(moe[at, :], wgu[e, :, 512 + c * COLS : 512 + c * COLS + COLS])
                a = g / (1.0 + jnp.exp(-g)) * u * gate2
                act[at, pl.ds(pl.multiple_of(e * 512 + c * COLS, COLS), COLS)] = a.astype(BF16)
            return carry

        lax.fori_loop(first, stop, expert_step, 0)

    quarter, eighth = half // 2, half // 8
    wide = 2 * COLS
    ring = [(across, (zz + 2) % 4), (up, (zz + 1) % 4), (down, (zz + 3) % 4)]

    def own_part(ref, n):
        return ref.at[n, pl.ds(pl.multiple_of(core * quarter + zz * eighth, eighth), eighth)]

    def l1_copy(n):
        return pltpu.make_async_remote_copy(p1s.at[n], p1r.at[n], l1_s.at[n], l1_r.at[n], device_id={"head": mate})

    def l2_copy(n, i):
        dev, z = ring[i]
        return pltpu.make_async_remote_copy(
            p2s.at[n, pl.ds(z * eighth, eighth)], p2r.at[n, i], l2_s.at[n, i], l2_r.at[n, i],
            device_id={"head": dev},
        )

    def ag_copy(n, h, dev, ss):
        at = outb.at[n, pl.ds((h % 2) * quarter + (h // 2) * eighth, eighth)]
        return pltpu.make_async_remote_copy(at, at, ss, ag_r.at[n, h], device_id={"head": dev})

    def out_copy(n):
        at = out_h.at[pl.ds((n // 2) * half, half), pl.ds((n % 2) * wide, wide)]
        return pltpu.make_async_copy(outb.at[n], at, out_sem.at[n])

    def stage_down(n):
        down_out[...] = dot(act[(n // 2) * half : (n // 2) * half + half, :], wd[:, (n % 2) * wide : (n % 2) * wide + wide])
        p1s[n] = down_out[pl.ds(pl.multiple_of((1 - core) * quarter, quarter), quarter), :].astype(BF16)
        l1_copy(n).start()
        keep[n] = down_out[pl.ds(pl.multiple_of(core * quarter, quarter), quarter), :]

    def stage_sum(n):
        l1_copy(n).wait_recv()
        t = keep[n] + p1r[n].astype(F32)
        p2s[n] = t.astype(BF16)
        for i in range(3):
            l2_copy(n, i).start()
        keep[n] = t

    def stage_final(n):
        t = keep[n, pl.ds(pl.multiple_of(zz * eighth, eighth), eighth), :]
        rows_at = pl.ds(pl.multiple_of((n // 2) * half + core * quarter + zz * eighth, eighth), eighth)
        t = t + hidden[rows_at, (n % 2) * wide : (n % 2) * wide + wide].astype(F32)
        for i in (1, 2, 0):
            l2_copy(n, i).wait_recv()
            t = t + p2r[n, i].astype(F32)
        own_part(outb, n)[...] = t.astype(BF16)
        for i in range(3):
            ag_copy(n, hh, ring[i][0], ag_s.at[n, i]).start()
        ag_copy(n, hh, mate, ag_f.at[n, 3]).start()

    def stage_pass(n):
        for i in (1, 2, 0):
            ag_copy(n, ring[i][0], mate, ag_s.at[n, i]).wait_recv()
            ag_copy(n, ring[i][0], mate, ag_f.at[n, i]).start()

    def stage_out(n):
        for z in range(4):
            ag_copy(n, ((zz + z) % 4) * 2 + 1 - core, mate, ag_s.at[n, 0]).wait_recv()
        out_copy(n).start()

    @pl.when(jnp.logical_not(early))
    def _():
        for k in by_distance:
            pg_copy(k).start()

    project(0)
    for e in range(1, 6):
        big[e].wait()
    cx_pass(1)
    experts(0, 0, 4)
    stage_down(0)
    stage_down(1)
    stage_sum(0)
    cx_finish(1)
    project(1)
    stage_sum(1)
    experts(1, 0, 2)
    stage_final(0)
    stage_final(1)
    experts(1, 2, 4)
    stage_down(2)
    stage_pass(0)
    stage_down(3)
    stage_pass(1)
    stage_sum(2)
    stage_sum(3)
    stage_out(0)
    stage_out(1)
    for stage in (stage_final, stage_pass, stage_out):
        stage(2)
        stage(3)

    pg_own.wait()
    for k in by_distance:
        src = torus_peer(k)
        pltpu.make_async_remote_copy(
            psend.at[pl.ds(0, 8)], precv.at[pl.ds(src * 8, 8)], pg_s.at[k], pg_r.at[src], device_id={"seq": src}
        ).wait_recv()
    for k in by_distance:
        pg_copy(k).wait_send()

    for i in range(max_sends):
        needed, c = kv_copy(i)

        @pl.when(needed)
        def _(c=c):
            c.wait_send()

    @pl.when(ships)
    def _():
        q_copy.wait_send()

    @pl.when(helps)
    def _():
        for c in part_copies:
            c.wait_send()

    for c in wo.started + cx.started:
        c.wait_send()
    for n in range(4):
        l1_copy(n).wait_send()
        for i in range(3):
            l2_copy(n, i).wait_send()
            ag_copy(n, hh, ring[i][0], ag_s.at[n, i]).wait_send()
            ag_copy(n, ring[i][0], mate, ag_f.at[n, i]).wait_send()
        ag_copy(n, hh, mate, ag_f.at[n, 3]).wait_send()
        out_copy(n).wait()


def finish_kernel(n_seq, sum_h, pages_h, rp_h, rd_h, out_h, relaid_h, rows_v, got, placed, rp, rd, in_sem, out_sem):
    me = lax.axis_index("seq")
    n_col = 8
    width = got.shape[1] // n_col
    tall = rows_v.shape[0] // 4
    tables = [pltpu.make_async_copy(rp_h, rp, in_sem.at[12]), pltpu.make_async_copy(rd_h, rd, in_sem.at[13])]
    for c in tables:
        c.start()

    def load(i):
        cols = pl.ds(i * width, width)
        return pltpu.make_async_copy(pages_h.at[:, cols], got.at[:, cols], in_sem.at[i])

    def store(i):
        cols = pl.ds(i * width, width)
        return pltpu.make_async_copy(placed.at[:, cols], relaid_h.at[:, cols], out_sem.at[i])

    def load_rows(i):
        at = pl.ds(i * tall, tall)
        return pltpu.make_async_copy(sum_h.at[at], rows_v.at[at], in_sem.at[n_col + i])

    def store_rows(i):
        at = pl.ds(i * tall, tall)
        return pltpu.make_async_copy(rows_v.at[at], out_h.at[at], out_sem.at[n_col + i])

    for i in range(n_col):
        load(i).start()
    for i in range(4):
        load_rows(i).start()
    for c in tables:
        c.wait()
    len_m = jnp.sum(jnp.where(rd[...] == me, rp[...].astype(F32), 0.0), axis=1, keepdims=True)
    s_of = lax.broadcasted_iota(jnp.int32, (16, 128), 1) // 8
    s_row = lax.broadcasted_iota(jnp.int32, (16, 128), 0)
    len_c = jnp.sum(jnp.where(s_row == s_of, len_m, 0.0), axis=0, keepdims=True)
    off_c = jnp.sum(jnp.where(s_row < s_of, len_m, 0.0), axis=0, keepdims=True)
    to_row = lax.broadcasted_iota(jnp.int32, (128, 128), 0).astype(F32)
    sub_c = (lax.broadcasted_iota(jnp.int32, (128, 128), 1) % 8).astype(F32)
    place = jnp.where((to_row == off_c + sub_c) & (sub_c < len_c), 1.0, 0.0).astype(BF16)
    for i in range(n_col):
        load(i).wait()
        cols = slice(i * width, (i + 1) * width)
        placed[:, cols] = dot(place, got[:, cols]).astype(BF16)
        store(i).start()
    for i in range(4):
        load_rows(i).wait()
        store_rows(i).start()
    for i in range(n_col):
        store(i).wait()
    for i in range(4):
        store_rows(i).wait()


def per_device(
    n_seq, tokens, attn_gain, w_query, key_weight, value_weight, w_out, moe_gain, w_router, w_gate_up, w_down,
    expert_ids, source_cache_pages, req_pages, req_dest,
):
    rows, width = tokens.shape
    n_pages, _, entries = source_cache_pages.shape
    tables = rotary_tables(rows * n_seq, 64)
    half = rows // 2
    v = pltpu.VMEM
    scratch = [
        v((rows, width), BF16), v((1, width), F32), v((width, 128), BF16), v((128, width), BF16),
        v((1, width), F32), v((32, width), BF16), v(w_gate_up.shape, BF16), v((2048, width), BF16),
        v((8, rows), jnp.int32), v((n_pages, entries), BF16), v((16, 16), jnp.int32), v((16, 16), jnp.int32),
        v((128, 128), F32), v((128, 128), F32), v((64, 128), F32), v((64, 128), F32),
        v((1024, width), BF16), v((rows, width), BF16), v((n_seq, rows, 128), BF16), v((2, 2, rows, 128), BF16),
        v((rows, 128), BF16), v((rows, 128), BF16), v((2, 2, rows, 128), F32), v((rows, 128), BF16),
        v((2, 8, rows), F32), v((rows, 128), BF16), v((2, 8, rows), F32), v((8, rows, 128), BF16), v((rows, width), BF16), v((rows, width), BF16),
        v((half, 512), F32), v((4, rows, 128), F32), v((rows, 2048), BF16),
        v((4, half // 2, 512), BF16), v((4, half // 2, 512), F32), v((4, half // 2, 512), BF16),
        v((4, half // 2, 512), BF16), v((4, 3, half // 8, 512), BF16), v((4, half, 512), BF16), v((128, entries), BF16),
    ]
    d = pltpu.SemaphoreType.DMA
    scratch += [
        d((21,)), d((n_seq,)), d((n_seq,)), d, d, d((2,)), d((2,)), d((n_seq,)), d((n_seq,)),
        d((14,)), d((8, 2)), d((14,)), d((8, 2)),
        d((4,)), d((4,)), d((4, 3)), d((4, 3)), d((4, 3)), d((4, 8)), d((4, 4)), d((4,)),
    ]
    args = (
        tokens, attn_gain.reshape(1, width), w_query, key_weight.T, value_weight.T, w_out, moe_gain.reshape(1, width),
        w_router.T, w_gate_up, w_down.reshape(2048, width), expert_ids.T, source_cache_pages.reshape(n_pages, entries),
        req_pages, req_dest, *[jnp.asarray(t) for t in tables],
    )
    any_spec = pl.BlockSpec(memory_space=pl.ANY)
    shapes = (jax.ShapeDtypeStruct((rows, width), BF16), jax.ShapeDtypeStruct((128, entries), BF16))
    summed, received = pl.pallas_call(
        functools.partial(kernel, n_seq),
        out_shape=shapes,
        in_specs=[any_spec] * len(args),
        out_specs=(any_spec, any_spec),
        scratch_shapes=scratch,
        compiler_params=pltpu.CompilerParams(
            collective_id=0, has_side_effects=True, vmem_limit_bytes=60 * 1024 * 1024
        ),
        name="layer",
    )(*args)
    layer_out, relaid = pl.pallas_call(
        functools.partial(finish_kernel, n_seq),
        out_shape=shapes,
        in_specs=[any_spec] * 4,
        out_specs=(any_spec, any_spec),
        scratch_shapes=[
            v((rows, width), BF16), v((128, entries), BF16), v((128, entries), BF16),
            v((16, 16), jnp.int32), v((16, 16), jnp.int32), d((14,)), d((12,)),
        ],
        compiler_params=pltpu.CompilerParams(vmem_limit_bytes=60 * 1024 * 1024),
        name="finish",
    )(summed, received, req_pages, req_dest)
    return layer_out, relaid.reshape(128, 1, entries)


def solution(mesh):
    in_specs = (
        P("seq", None), P(), P(None, "head"), P(None, "head"), P(None, "head"), P("head", None), P(), P(),
        P("head", None, None), P("head", None, None), P("seq", None), P("seq", "head", None), P(), P(),
    )
    out_specs = (P("seq", None), P("seq", "head", None))
    return jax.shard_map(
        functools.partial(per_device, mesh.shape["seq"]),
        mesh=mesh, in_specs=in_specs, out_specs=out_specs, check_vma=False,
    )
```

```python
import functools

import jax
import jax.numpy as jnp
import numpy as np
from jax import lax
from jax.experimental import pallas as pl
from jax.experimental.pallas import tpu as pltpu
from jax.sharding import PartitionSpec as P

HD = 64
LANES = 128
COLS = 256
F32 = jnp.float32
BF16 = jnp.bfloat16
NT = (((1,), (1,)), ((), ()))

TASKS = (
    (),
    ((0, 0),),
    ((1, 1), (1, 2), (0, 1), (1, 3), (1, 6), (1, 0), (1, 5), (0, 0), (1, 4),),
    ((1, 0), (1, 3), (1, 7), (1, 1), (0, 0), (0, 1), (0, 2), (1, 4),),
    ((1, 0), (1, 3), (0, 0), (1, 7), (1, 8), (0, 3), (1, 1), (0, 1), (1, 2), (0, 2),),
    ((1, 1), (1, 2), (1, 5), (0, 1), (1, 4), (1, 6), (0, 2), (0, 4), (0, 3), (0, 0),),
    ((1, 5), (1, 3), (0, 3), (0, 2), (1, 0), (0, 0),),
    ((1, 6), (0, 6), (1, 2), (1, 5), (0, 2), (1, 8), (0, 4), (1, 1), (0, 1),),
    ((1, 4), (1, 8), (1, 11), (1, 12), (1, 9), (1, 7), (0, 7), (1, 0), (0, 0), (0, 3),),
    ((1, 5), (0, 5), (1, 4), (0, 4), (1, 1), (0, 6),),
    ((0, 9), (0, 6), (0, 5), (0, 8), (0, 2),),
    ((0, 10), (0, 9), (0, 7), (0, 3), (0, 4), (0, 0),),
    ((1, 12), (1, 0), (1, 8), (0, 0), (1, 4), (0, 11), (0, 4), (0, 9), (1, 1), (0, 1), (0, 7), (0, 5),),
    ((1, 10), (1, 8), (0, 10), (1, 2), (1, 3), (0, 2), (0, 3), (1, 6), (0, 5), (0, 1), (0, 6),),
    ((0, 13), (0, 10), (0, 9), (0, 11), (0, 3), (0, 2), (0, 6), (0, 7), (0, 5),),
    ((0, 11), (0, 12), (0, 14), (0, 13), (0, 8), (0, 10), (0, 7), (0, 9),),
)
SENDS = (
    (3, 4, 12, 2, 8, 1, 6, 5, 11,),
    (2, 5, 3, 4, 9, 12, 13, 7,),
    (5, 7, 13, 3, 6, 14, 4, 10,),
    (2, 4, 6, 13, 11, 14, 5, 8,),
    (5, 8, 9, 12, 3, 7, 2, 11,),
    (6, 9, 7, 2, 10, 13, 12, 14,),
    (7, 2, 5, 10, 13, 9, 14,),
    (3, 4, 8, 11, 15, 12, 14,),
    (12, 4, 13, 7, 10, 15,),
    (8, 10, 11, 12, 14, 15,),
    (13, 11, 14, 15,),
    (8, 15, 12, 14,),
    (8, 15,),
    (14, 15,),
    (15,),
    (),
)
HELPER = (-1, -1, -1, -1, -1, -1, 9, 6, 5, 4, 3, 7, 13, 8, 12, 2)


def pack_words(lists, per_word, bits):
    words = -(-max(len(x) for x in lists) // per_word)
    return [
        [sum(code << bits * k for k, code in enumerate(x[w * per_word : (w + 1) * per_word])) for x in lists]
        for w in range(words)
    ]


def task_codes(d):
    seen, codes = {d}, []
    for w, b in TASKS[d]:
        codes.append((b not in seen) * 32 + w * 16 + b)
        seen.add(b)
    return codes


def rotary_tables(tokens, rows):
    lane_freq = np.arange(LANES) % (HD // 2)
    freq = 10000.0 ** (lane_freq * (-2.0 / HD))
    coarse = np.arange(tokens // rows)[:, None] * float(rows) * freq[None, :]
    fine = np.arange(rows)[:, None] * freq[None, :]
    table = [np.cos(coarse), np.sin(coarse), np.cos(fine), np.sin(fine)]
    return [part.astype(np.float32) for part in table]


def dot(a, b, dims=None):
    if dims is None:
        return jnp.dot(a, b, preferred_element_type=F32)
    return lax.dot_general(a, b, dims, preferred_element_type=F32)


def kernel(
    n_seq,
    tok_h, again_h, wq_h, wkt_h, wvt_h, wo_h, mgain_h, wrt_h, wgu_h, wd_h, ids_h, pages_h, rp_h, rd_h,
    cc_h, cs_h, fc_h, fs_h,
    out_h, precv,
    tok, again, wq, wkvt, mgain, wrt, wgu, wd, ids, pages, rp, rd, cc, cs, fc, fs,
    woutg, normed, kvbuf, qbuf, qpack, qrecv, acc, partn, partd, prtn, prtd, ctxg, hidden, moe, down_out, gb, act,
    p1s, keep, p1r, p2s, p2r, outb, psend,
    sem_in, kv_s, kv_r, q_s, q_r, pt_s, pt_r, pg_s, pg_r, wo_s, wo_r, cx_s, cx_r,
    l1_s, l1_r, l2_s, l2_r, ag_s, ag_r, ag_f, out_sem,
):
    me = lax.axis_index("seq")
    hh = lax.axis_index("head")
    zz = hh // 2
    core = hh % 2
    mate = hh + 1 - 2 * core
    rows = tok.shape[0]
    half = rows // 2

    def pick(values):
        out = values[0]
        for i in range(1, n_seq):
            out = jnp.where(me == i, values[i], out)
        return out

    helps_whom = [HELPER.index(d) if d in HELPER else -1 for d in range(n_seq)]
    my_helper, my_guest = pick(HELPER), pick(helps_whom)
    ships, helps = my_helper >= 0, my_guest >= 0
    n_tasks = pick([len(t) for t in TASKS])
    n_sends = pick([len(t) for t in SENDS])
    task_words = [pick(w) for w in pack_words([task_codes(d) for d in range(n_seq)], 5, 6)]
    send_words = [pick(w) for w in pack_words(SENDS, 7, 4)]
    max_sends = max(len(t) for t in SENDS)
    guest_steps = [[i for i, t in enumerate(TASKS[d]) if t[0] == 1] or [-1] for d in range(n_seq)]
    first_guest, last_guest = pick([g[0] for g in guest_steps]), pick([g[-1] for g in guest_steps])

    barrier = pltpu.get_barrier_semaphore()
    for k in range(1, n_seq):
        pl.semaphore_signal(barrier, inc=1, device_id={"seq": (me + k) % n_seq})
    for k in range(1, 8):
        pl.semaphore_signal(barrier, inc=1, device_id={"head": (hh + k) % 8})

    loads = [
        (tok_h, tok), (again_h, again), (wq_h, wq), (wkt_h, wkvt.at[pl.ds(0, HD)]),
        (wvt_h, wkvt.at[pl.ds(HD, HD)]), (cc_h, cc), (cs_h, cs), (fc_h, fc), (fs_h, fs),
        (pages_h, pages), (rp_h, rp), (rd_h, rd),
        (mgain_h, mgain), (wrt_h, wrt), (ids_h, ids),
    ]
    copies = [pltpu.make_async_copy(src, dst, sem_in.at[i]) for i, (src, dst) in enumerate(loads)]
    n0 = len(copies)
    big = [pltpu.make_async_copy(wo_h, woutg.at[pl.ds(hh * 128, 128)], sem_in.at[n0])]
    for e in range(4):
        big.append(pltpu.make_async_copy(wgu_h.at[e], wgu.at[e], sem_in.at[n0 + 1 + e]))
    big.append(pltpu.make_async_copy(wd_h, wd, sem_in.at[n0 + 5]))
    for c in copies:
        c.start()
    for c in big:
        c.start()

    for i in (0, 1):
        copies[i].wait()
    for r in range(0, rows, 128):
        x = tok[r : r + 128, :].astype(F32)
        scale = lax.rsqrt(jnp.mean(x * x, axis=1, keepdims=True) + 1e-05)
        normed[r : r + 128, :] = (x * scale * again[...]).astype(BF16)
    for i in range(2, 9):
        copies[i].wait()

    q = dot(normed[...], wq[...])
    kv = dot(normed[...], wkvt[...], NT)
    lane = lax.broadcasted_iota(jnp.int32, (64, LANES), 1)
    first = (lane % HD) < HD // 2
    low = lane < HD
    own_kv = kvbuf.at[me]
    ccb = cc[pl.ds(pl.multiple_of(me * 8, 8), 8), :]
    csb = cs[pl.ds(pl.multiple_of(me * 8, 8), 8), :]
    for g in range(rows // 64):
        ca = ccb[g : g + 1, :]
        sa = csb[g : g + 1, :]
        cosv = ca * fc[...] - sa * fs[...]
        sinv = sa * fc[...] + ca * fs[...]
        sinv = jnp.where(first, -sinv, sinv)
        sl = slice(g * 64, g * 64 + 64)
        qg = q[sl]
        kg = kv[sl]
        qsw = jnp.where(first, pltpu.roll(qg, 96, 1), pltpu.roll(qg, 32, 1))
        ksw = jnp.where(first, pltpu.roll(kg, 96, 1), pltpu.roll(kg, 32, 1))
        qr = qg * cosv + qsw * sinv
        kr = jnp.where(low, kg * cosv + ksw * sinv, kg)
        kvbuf[me, sl, :] = kr.astype(BF16)
        qpack[sl, :] = qr.astype(BF16)
        qbuf[0, 0, sl, :] = jnp.where(low, qr, 0.0).astype(BF16)
        qbuf[0, 1, sl, :] = jnp.where(low, pltpu.roll(qr, HD, 1), 0.0).astype(BF16)

    pl.semaphore_wait(barrier, n_seq - 1 + 7)

    def kv_copy(i):
        peer = (send_words[i // 7] // 16 ** (i % 7)) % 16
        return i < n_sends, pltpu.make_async_remote_copy(
            own_kv, kvbuf.at[me], kv_s.at[i], kv_r.at[me], device_id={"seq": peer}
        )

    def torus_peer(k):
        return ((me // 4 + k // 4) % 4) * 4 + (me % 4 + k % 4) % 4

    by_distance = sorted(range(1, n_seq), key=lambda k: (min(k // 4, 4 - k // 4) + min(k % 4, 4 - k % 4), k))
    q_copy = pltpu.make_async_remote_copy(qpack, qrecv, q_s, q_r, device_id={"seq": my_helper})

    @pl.when(ships)
    def _():
        q_copy.start()

    for i in range(max_sends):
        needed, c = kv_copy(i)

        @pl.when(needed)
        def _(c=c):
            c.start()

    up = ((zz + 1) % 4) * 2 + core
    down = ((zz + 3) % 4) * 2 + core
    across = ((zz + 2) % 4) * 2 + core

    class Gather:
        def __init__(self, piece, send_sems, recv_sems):
            self.piece, self.ss, self.rs, self.started = piece, send_sems, recv_sems, []

        def copy(self, src, part, dev, k, from_ref=None):
            ref = self.piece(src, part)
            return pltpu.make_async_remote_copy(
                ref if from_ref is None else from_ref, ref, self.ss(k), self.rs(src, part), device_id={"head": dev}
            )

        def send(self, src, part, dev, from_ref=None):
            c = self.copy(src, part, dev, len(self.started), from_ref)
            c.start()
            self.started.append(c)

        def wait(self, src, part):
            self.copy(src, part, mate, 0).wait_recv()

        def begin(self, own=(None, None)):
            for part, dev in ((0, up), (1, down), (1, up), (0, down), (0, mate), (1, mate)):
                self.send(hh, part, dev, own[part])

        def relay(self):
            for src, part, nxt in ((down, 0, up), (up, 1, down), (down, 1, None), (up, 0, None)):
                self.wait(src, part)
                if nxt is not None:
                    self.send(src, part, nxt)
                self.send(src, part, mate)

        def relay_across(self):
            for part in (0, 1):
                self.wait(across, part)
                self.send(across, part, mate)

        def finish(self):
            for z in range(4):
                for part in (0, 1):
                    self.wait(((zz + z) % 4) * 2 + 1 - core, part)

    wo = Gather(
        lambda h, p: woutg.at[pl.ds(h * 128 + p * 64, 64)], lambda k: wo_s.at[k], lambda h, p: wo_r.at[h, p]
    )
    wo.begin((wo_h.at[pl.ds(0, 64)], wo_h.at[pl.ds(64, 64)]))

    for i in range(9, 12):
        copies[i].wait()
    srow = lax.broadcasted_iota(jnp.int32, (16, 16), 0)
    mine = srow == me
    own_pages = jnp.sum(jnp.where(mine, rp[...].astype(F32), 0.0), axis=0, keepdims=True)
    own_dest = jnp.sum(jnp.where(mine, rd[...].astype(F32), 0.0), axis=0, keepdims=True)
    slot = lax.broadcasted_iota(jnp.int32, (128, 16), 0)
    req = lax.broadcasted_iota(jnp.int32, (128, 16), 1).astype(F32)
    match = own_dest == (slot // 8).astype(F32)
    send_len = jnp.sum(jnp.where(match, own_pages, 0.0), axis=1, keepdims=True)
    send_req = jnp.sum(jnp.where(match, req, 0.0), axis=1, keepdims=True)
    send_start = jnp.sum(jnp.where(req < send_req, own_pages, 0.0), axis=1, keepdims=True)
    sub = (lax.broadcasted_iota(jnp.int32, (128, 64), 0) % 8).astype(F32)
    src_row = lax.broadcasted_iota(jnp.int32, (128, 64), 1).astype(F32)
    pack = jnp.where((src_row == send_start + sub) & (sub < send_len), 1.0, 0.0).astype(BF16)

    def pack_step(i, carry):
        cols = pl.ds(pl.multiple_of(i * 1024, 1024), 1024)
        psend[:, cols] = dot(pack, pages[:, cols]).astype(BF16)
        return carry

    lax.fori_loop(0, 8, pack_step, 0)
    pg_own = pltpu.make_async_copy(psend.at[pl.ds(me * 8, 8)], precv.at[pl.ds(me * 8, 8)], pg_s.at[0])
    pg_own.start()

    def pg_copy(k):
        peer = torus_peer(k)
        return pltpu.make_async_remote_copy(
            psend.at[pl.ds(peer * 8, 8)], precv.at[pl.ds(me * 8, 8)], pg_s.at[k], pg_r.at[me],
            device_id={"seq": peer},
        )

    def attend(w, h, r0, nr, kblk, v1, diag):
        qt = qbuf[w, h, r0 : r0 + nr, :]
        s = dot(qt, kblk, NT)
        wts = jnp.exp(30.0 * jnp.tanh(s * (1.0 / 240.0)))
        if diag:
            tri = lax.broadcasted_iota(jnp.int32, s.shape, 1) <= lax.broadcasted_iota(jnp.int32, s.shape, 0)
            wts = jnp.where(tri, wts, 0.0)
        return dot(wts.astype(BF16), v1)

    def ones_in(kv_part):
        keep_low = lax.broadcasted_iota(jnp.int32, kv_part.shape, 1) < HD
        return jnp.where(keep_low, jnp.ones_like(kv_part), kv_part)

    ka, kb = kvbuf[me, :half, :], kvbuf[me, half:, :]
    va, vb = ones_in(ka), ones_in(kb)
    for h in range(2):
        acc[0, h, :half, :] = attend(0, h, 0, half, ka, va, True)
        acc[0, h, half:, :] = attend(0, h, half, half, ka, va, False) + attend(0, h, half, half, kb, vb, True)
    acc[1] = jnp.zeros_like(acc[1])

    def block(w, b):
        kblk = kvbuf[b]
        v1 = ones_in(kblk)
        tiles = [(h, k0) for h in range(2) for k0 in (0, half)]

        def scores(h, k0):
            return dot(qbuf[w, h], kblk[k0 : k0 + half], NT)

        ahead = scores(*tiles[0])
        for i, (h, k0) in enumerate(tiles):
            s, ahead = ahead, scores(*tiles[i + 1]) if i + 1 < len(tiles) else None
            wts = jnp.exp(30.0 * jnp.tanh(s * (1.0 / 240.0)))
            acc[w, h] += dot(wts.astype(BF16), v1[k0 : k0 + half])

    def kv_wait(b):
        pltpu.make_async_remote_copy(
            own_kv, kvbuf.at[b], kv_s.at[0], kv_r.at[b], device_id={"seq": my_helper}
        ).wait_recv()

    part_copies = [
        pltpu.make_async_remote_copy(src, dst, pt_s.at[i], pt_r.at[i], device_id={"seq": my_guest})
        for i, (src, dst) in enumerate(((partn, prtn), (partd, prtd)))
    ]
    low_c = lax.broadcasted_iota(jnp.int32, (rows, LANES), 1) < HD

    def task_step(i, carry):
        word = task_words[0]
        for w in range(1, len(task_words)):
            word = jnp.where(i >= 5 * w, task_words[w], word)
        code = lax.shift_right_logical(word, 6 * (i % 5)) % 64
        b = code % 16

        @pl.when(code >= 32)
        def _():
            kv_wait(b)

        @pl.when(i == first_guest)
        def _():
            q_copy.wait_recv()
            qr = qrecv[...]
            zero = jnp.zeros_like(qr)
            qbuf[1, 0] = jnp.where(low_c, qr, zero)
            qbuf[1, 1] = jnp.where(low_c, pltpu.roll(qr.astype(F32), HD, 1).astype(BF16), zero)

        block((code // 16) % 2, b)

        @pl.when(i == last_guest)
        def _():
            partn[...] = jnp.where(low_c, pltpu.roll(acc[1, 0], HD, 1), acc[1, 1]).astype(BF16)
            for h in range(2):
                partd[h] = jnp.transpose(acc[1, h])[0:8, :]
            for c in part_copies:
                c.start()

        return carry

    lax.fori_loop(0, n_tasks // 2, task_step, 0)
    wo.relay()
    lax.fori_loop(n_tasks // 2, n_tasks, task_step, 0)
    wo.relay_across()
    early = pick([d in (2, 3, 7, 10, 11, 12, 13, 14, 15) for d in range(n_seq)])

    @pl.when(early)
    def _():
        for k in by_distance:
            pg_copy(k).start()

    acc[1, 0] = jnp.where(low_c, pltpu.roll(acc[0, 0], HD, 1), acc[0, 1])
    acc[1, 1] = jnp.where(low_c, acc[0, 0], pltpu.roll(acc[0, 1], HD, 1))

    @pl.when(ships)
    def _():
        for c in part_copies:
            c.wait_recv()
        acc[1, 0] += prtn[...].astype(F32)
        den = [jnp.transpose(jnp.broadcast_to(prtd[h, 0:1, :], (LANES, rows))) for h in range(2)]
        acc[1, 1] += jnp.where(low_c, den[0], den[1])

    ctxg[hh] = (acc[1, 0] / acc[1, 1]).astype(BF16)

    cx = Gather(lambda h, p: ctxg.at[h, pl.ds(p * half, half)], lambda k: cx_s.at[k], lambda h, p: cx_r.at[h, p])
    for part in (0, 1):
        for dev in (across, up, down, mate):
            cx.send(hh, part, dev)
    big[0].wait()
    for i in range(12, 15):
        copies[i].wait()

    def cx_pass(part):
        for src in (up, down, across):
            cx.wait(src, part)
            cx.send(src, part, mate)

    def cx_finish(part):
        for z in range(4):
            cx.wait(((zz + z) % 4) * 2 + 1 - core, part)

    wo.finish()
    cx_pass(0)
    cx_finish(0)

    def project(r):
        at = slice(r * half, r * half + half)
        x = jnp.concatenate([ctxg[i, at, :] for i in range(8)], axis=1)
        hid = (tok[at, :].astype(F32) + dot(x, woutg[...])).astype(BF16)
        hidden[at, :] = hid
        hf = hid.astype(F32)
        scale = lax.rsqrt(jnp.mean(hf * hf, axis=1, keepdims=True) + 1e-05)
        moe[at, :] = (hf * scale * mgain[...]).astype(BF16)
        logits = dot(wrt[...], moe[at, :], NT)
        expert = lax.broadcasted_iota(jnp.int32, logits.shape, 0)
        chosen = expert == ids[0:1, at]
        for k in range(1, 8):
            chosen = chosen | (expert == ids[k : k + 1, at])
        raised = jnp.where(chosen, jnp.exp(logits), 0.0)
        gates = raised / jnp.sum(raised, axis=0, keepdims=True)
        gcol = jnp.transpose(jnp.concatenate([gates, jnp.zeros((96, half), F32)], axis=0))
        lane_r = lax.broadcasted_iota(jnp.int32, (half, LANES), 1)
        for e in range(4):
            picked = jnp.sum(jnp.where(lane_r == hh * 4 + e, gcol, 0.0), axis=1, keepdims=True)
            gb[e, at, :] = jnp.broadcast_to(picked, (half, LANES))

    def experts(r, first, stop):
        at = slice(r * half, r * half + half)

        def expert_step(e, carry):
            gate2 = jnp.concatenate([gb[e, at, :], gb[e, at, :]], axis=1)
            for c in range(2):
                g = dot(moe[at, :], wgu[e, :, c * COLS : c * COLS + COLS])
                u = dot(moe[at, :], wgu[e, :, 512 + c * COLS : 512 + c * COLS + COLS])
                a = g / (1.0 + jnp.exp(-g)) * u * gate2
                act[at, pl.ds(pl.multiple_of(e * 512 + c * COLS, COLS), COLS)] = a.astype(BF16)
            return carry

        lax.fori_loop(first, stop, expert_step, 0)

    quarter, eighth = half // 2, half // 8
    wide = 2 * COLS
    ring = [(across, (zz + 2) % 4), (up, (zz + 1) % 4), (down, (zz + 3) % 4)]

    def own_part(ref, n):
        return ref.at[n, pl.ds(pl.multiple_of(core * quarter + zz * eighth, eighth), eighth)]

    def l1_copy(n):
        return pltpu.make_async_remote_copy(p1s.at[n], p1r.at[n], l1_s.at[n], l1_r.at[n], device_id={"head": mate})

    def l2_copy(n, i):
        dev, z = ring[i]
        return pltpu.make_async_remote_copy(
            p2s.at[n, pl.ds(z * eighth, eighth)], p2r.at[n, i], l2_s.at[n, i], l2_r.at[n, i],
            device_id={"head": dev},
        )

    def ag_copy(n, h, dev, ss):
        at = outb.at[n, pl.ds((h % 2) * quarter + (h // 2) * eighth, eighth)]
        return pltpu.make_async_remote_copy(at, at, ss, ag_r.at[n, h], device_id={"head": dev})

    def out_copy(n):
        at = out_h.at[pl.ds((n // 2) * half, half), pl.ds((n % 2) * wide, wide)]
        return pltpu.make_async_copy(outb.at[n], at, out_sem.at[n])

    def stage_down(n):
        down_out[...] = dot(act[(n // 2) * half : (n // 2) * half + half, :], wd[:, (n % 2) * wide : (n % 2) * wide + wide])
        p1s[n] = down_out[pl.ds(pl.multiple_of((1 - core) * quarter, quarter), quarter), :].astype(BF16)
        l1_copy(n).start()
        keep[n] = down_out[pl.ds(pl.multiple_of(core * quarter, quarter), quarter), :]

    def stage_sum(n):
        l1_copy(n).wait_recv()
        t = keep[n] + p1r[n].astype(F32)
        p2s[n] = t.astype(BF16)
        for i in range(3):
            l2_copy(n, i).start()
        keep[n] = t

    def stage_final(n):
        t = keep[n, pl.ds(pl.multiple_of(zz * eighth, eighth), eighth), :]
        rows_at = pl.ds(pl.multiple_of((n // 2) * half + core * quarter + zz * eighth, eighth), eighth)
        t = t + hidden[rows_at, (n % 2) * wide : (n % 2) * wide + wide].astype(F32)
        for i in (1, 2, 0):
            l2_copy(n, i).wait_recv()
            t = t + p2r[n, i].astype(F32)
        own_part(outb, n)[...] = t.astype(BF16)
        for i in range(3):
            ag_copy(n, hh, ring[i][0], ag_s.at[n, i]).start()
        ag_copy(n, hh, mate, ag_f.at[n, 3]).start()

    def stage_pass(n):
        for i in (1, 2, 0):
            ag_copy(n, ring[i][0], mate, ag_s.at[n, i]).wait_recv()
            ag_copy(n, ring[i][0], mate, ag_f.at[n, i]).start()

    def stage_out(n):
        for z in range(4):
            ag_copy(n, ((zz + z) % 4) * 2 + 1 - core, mate, ag_s.at[n, 0]).wait_recv()
        out_copy(n).start()

    @pl.when(jnp.logical_not(early))
    def _():
        for k in by_distance:
            pg_copy(k).start()

    project(0)
    for e in range(1, 6):
        big[e].wait()
    experts(0, 0, 2)
    cx_pass(1)
    experts(0, 2, 4)
    stage_down(0)
    stage_down(1)
    stage_sum(0)
    cx_finish(1)
    project(1)
    stage_sum(1)
    experts(1, 0, 2)
    stage_final(0)
    stage_final(1)
    experts(1, 2, 4)
    stage_down(2)
    stage_pass(0)
    stage_down(3)
    stage_pass(1)
    stage_sum(2)
    stage_sum(3)
    stage_out(0)
    stage_out(1)
    for stage in (stage_final, stage_pass, stage_out):
        stage(2)
        stage(3)

    pg_own.wait()
    for k in by_distance:
        src = torus_peer(k)
        pltpu.make_async_remote_copy(
            psend.at[pl.ds(0, 8)], precv.at[pl.ds(src * 8, 8)], pg_s.at[k], pg_r.at[src], device_id={"seq": src}
        ).wait_recv()
    for k in by_distance:
        pg_copy(k).wait_send()

    for i in range(max_sends):
        needed, c = kv_copy(i)

        @pl.when(needed)
        def _(c=c):
            c.wait_send()

    @pl.when(ships)
    def _():
        q_copy.wait_send()

    @pl.when(helps)
    def _():
        for c in part_copies:
            c.wait_send()

    for c in wo.started + cx.started:
        c.wait_send()
    for n in range(4):
        l1_copy(n).wait_send()
        for i in range(3):
            l2_copy(n, i).wait_send()
            ag_copy(n, hh, ring[i][0], ag_s.at[n, i]).wait_send()
            ag_copy(n, ring[i][0], mate, ag_f.at[n, i]).wait_send()
        ag_copy(n, hh, mate, ag_f.at[n, 3]).wait_send()
        out_copy(n).wait()


def finish_kernel(n_seq, sum_h, pages_h, rp_h, rd_h, out_h, relaid_h, placed, rp, rd, in_sem, out_sem):
    me = lax.axis_index("seq")
    n_col = 8
    width = placed.shape[1] // n_col
    tall = sum_h.shape[0] // 4
    tables = [pltpu.make_async_copy(rp_h, rp, in_sem.at[12]), pltpu.make_async_copy(rd_h, rd, in_sem.at[13])]
    for c in tables:
        c.start()

    def store(i):
        cols = pl.ds(i * width, width)
        return pltpu.make_async_copy(placed.at[:, cols], relaid_h.at[:, cols], out_sem.at[i])

    def store_rows(i):
        at = pl.ds(i * tall, tall)
        return pltpu.make_async_copy(sum_h.at[at], out_h.at[at], out_sem.at[n_col + i])

    for i in range(4):
        store_rows(i).start()
    for c in tables:
        c.wait()
    len_m = jnp.sum(jnp.where(rd[...] == me, rp[...].astype(F32), 0.0), axis=1, keepdims=True)
    s_of = lax.broadcasted_iota(jnp.int32, (16, 128), 1) // 8
    s_row = lax.broadcasted_iota(jnp.int32, (16, 128), 0)
    len_c = jnp.sum(jnp.where(s_row == s_of, len_m, 0.0), axis=0, keepdims=True)
    off_c = jnp.sum(jnp.where(s_row < s_of, len_m, 0.0), axis=0, keepdims=True)
    to_row = lax.broadcasted_iota(jnp.int32, (128, 128), 0).astype(F32)
    sub_c = (lax.broadcasted_iota(jnp.int32, (128, 128), 1) % 8).astype(F32)
    place = jnp.where((to_row == off_c + sub_c) & (sub_c < len_c), 1.0, 0.0).astype(BF16)
    for i in range(n_col):
        cols = slice(i * width, (i + 1) * width)
        placed[:, cols] = dot(place, pages_h[:, cols]).astype(BF16)
        store(i).start()
    for i in range(n_col):
        store(i).wait()
    for i in range(4):
        store_rows(i).wait()


def per_device(
    n_seq, tokens, attn_gain, w_query, key_weight, value_weight, w_out, moe_gain, w_router, w_gate_up, w_down,
    expert_ids, source_cache_pages, req_pages, req_dest,
):
    rows, width = tokens.shape
    n_pages, _, entries = source_cache_pages.shape
    tables = rotary_tables(rows * n_seq, 64)
    half = rows // 2
    v = pltpu.VMEM
    scratch = [
        v((rows, width), BF16), v((1, width), F32), v((width, 128), BF16), v((128, width), BF16),
        v((1, width), F32), v((32, width), BF16), v(w_gate_up.shape, BF16), v((2048, width), BF16),
        v((8, rows), jnp.int32), v((n_pages, entries), BF16), v((16, 16), jnp.int32), v((16, 16), jnp.int32),
        v((128, 128), F32), v((128, 128), F32), v((64, 128), F32), v((64, 128), F32),
        v((1024, width), BF16), v((rows, width), BF16), v((n_seq, rows, 128), BF16), v((2, 2, rows, 128), BF16),
        v((rows, 128), BF16), v((rows, 128), BF16), v((2, 2, rows, 128), F32), v((rows, 128), BF16),
        v((2, 8, rows), F32), v((rows, 128), BF16), v((2, 8, rows), F32), v((8, rows, 128), BF16), v((rows, width), BF16), v((rows, width), BF16),
        v((half, 512), F32), v((4, rows, 128), F32), v((rows, 2048), BF16),
        v((4, half // 2, 512), BF16), v((4, half // 2, 512), F32), v((4, half // 2, 512), BF16),
        v((4, half // 2, 512), BF16), v((4, 3, half // 8, 512), BF16), v((4, half, 512), BF16), v((128, entries), BF16),
    ]
    d = pltpu.SemaphoreType.DMA
    scratch += [
        d((21,)), d((n_seq,)), d((n_seq,)), d, d, d((2,)), d((2,)), d((n_seq,)), d((n_seq,)),
        d((14,)), d((8, 2)), d((14,)), d((8, 2)),
        d((4,)), d((4,)), d((4, 3)), d((4, 3)), d((4, 3)), d((4, 8)), d((4, 4)), d((4,)),
    ]
    args = (
        tokens, attn_gain.reshape(1, width), w_query, key_weight.T, value_weight.T, w_out, moe_gain.reshape(1, width),
        w_router.T, w_gate_up, w_down.reshape(2048, width), expert_ids.T, source_cache_pages.reshape(n_pages, entries),
        req_pages, req_dest, *[jnp.asarray(t) for t in tables],
    )
    any_spec = pl.BlockSpec(memory_space=pltpu.HBM)
    vmem_spec = pl.BlockSpec(memory_space=pltpu.VMEM)
    shapes = (jax.ShapeDtypeStruct((rows, width), BF16), jax.ShapeDtypeStruct((128, entries), BF16))
    summed, received = pl.pallas_call(
        functools.partial(kernel, n_seq),
        out_shape=shapes,
        in_specs=[any_spec] * len(args),
        out_specs=(vmem_spec, vmem_spec),
        scratch_shapes=scratch,
        compiler_params=pltpu.CompilerParams(
            collective_id=0, has_side_effects=True, vmem_limit_bytes=46137344
        ),
        name="layer",
    )(*[pltpu.with_memory_space_constraint(a, pltpu.HBM) for a in args])
    layer_out, relaid = pl.pallas_call(
        functools.partial(finish_kernel, n_seq),
        out_shape=shapes,
        in_specs=[vmem_spec, vmem_spec, any_spec, any_spec],
        out_specs=(any_spec, any_spec),
        scratch_shapes=[
            v((128, entries), BF16),
            v((16, 16), jnp.int32), v((16, 16), jnp.int32), d((14,)), d((12,)),
        ],
        compiler_params=pltpu.CompilerParams(vmem_limit_bytes=46137344),
        name="finish",
    )(summed, received, *[pltpu.with_memory_space_constraint(a, pltpu.HBM) for a in (req_pages, req_dest)])
    return layer_out, relaid.reshape(128, 1, entries)


def solution(mesh):
    in_specs = (
        P("seq", None), P(), P(None, "head"), P(None, "head"), P(None, "head"), P("head", None), P(), P(),
        P("head", None, None), P("head", None, None), P("seq", None), P("seq", "head", None), P(), P(),
    )
    out_specs = (P("seq", None), P("seq", "head", None))
    return jax.shard_map(
        functools.partial(per_device, mesh.shape["seq"]),
        mesh=mesh, in_specs=in_specs, out_specs=out_specs, check_vma=False,
    )
```
